32 devices in a mesh: groups: 2 (over y), ctx: 16 (over z, x, core).
Axes of the slice: x: 2, y: 2, z: 4, core: 2. Of those that a mesh axis runs over, the one named last changes fastest.
Arguments:
- queries: bfloat16 [8192, 4096], P(('groups', 'ctx')), parts along dimension 0, may hold values from -13 to 13
- all_key_states: bfloat16 [8192, 512], P(('groups', 'ctx')), parts along dimension 0, may hold values from -9.5 to 9.5
- all_value_states: bfloat16 [8192, 512], P(('groups', 'ctx')), parts along dimension 0, may hold values from -6 to 6
- selected: int32 [32, 2], P(('groups', 'ctx')), parts along dimension 0, may hold values from 0 to 14, as said below
Outputs:
- attended: bfloat16 [8192, 4096], P(('groups', 'ctx')), parts along dimension 0
The draws below stay inside these ranges and needn't reach their ends.
There are 2 independent parts, one for each index of `groups`. The reference program is written for one: setup_inputs(seed, part) draws one part's arguments, and reference() takes and returns one part's arrays. A program takes and returns all parts, laid end to end along the dimension named above; each array names one. Nothing has to cross between parts.
Inputs may be any that keep to these rules, and one draw needn't show every extreme that they name: `selected`: for block i >= 2 the two entries of row i are different blocks below i; rows 0 and 1 hold 0 and 0; the last block's first entry is 14.
All inputs are finite; a program needn't handle non-finite values.
Results may differ from the reference program's by a relative error of at most 0.004.
Values may be sent and summed in bfloat16 or wider, within the bound.
A program may use at most 64 MiB of HBM per device.

```python
import math
import jax
import jax.numpy as jnp
from jax import lax

QUERY_HEADS = 32
KEY_VALUE_HEADS = 4
HEAD_SIZE = 128
BLOCK_TOKENS = 256
NBLK = 16
CONTEXT_TOKENS = 4096


def draw_queries(key, part):
    random_component = jnp.clip(jax.random.normal(jax.random.fold_in(key, 1), (CONTEXT_TOKENS, QUERY_HEADS, HEAD_SIZE), jnp.float32), -4.0, 4.0) * 1.5
    return random_component.reshape(CONTEXT_TOKENS, QUERY_HEADS * HEAD_SIZE).astype(jnp.bfloat16)


def draw_all_key_states(key, part):
    random_component = jnp.clip(jax.random.normal(jax.random.fold_in(key, 4), (CONTEXT_TOKENS, KEY_VALUE_HEADS, HEAD_SIZE), jnp.float32), -6.0, 6.0)
    return random_component.reshape(CONTEXT_TOKENS, KEY_VALUE_HEADS * HEAD_SIZE).astype(jnp.bfloat16)


def draw_selected(key, part):
    block_position = jnp.arange(NBLK, dtype=jnp.int32)
    first_pick = jax.random.randint(jax.random.fold_in(key, 11), (NBLK,), 0, jnp.maximum(block_position, 1))
    first_pick = jnp.where(block_position == NBLK - 1, block_position - 1, first_pick)
    second_pick = jax.random.randint(jax.random.fold_in(key, 12), (NBLK,), 0, jnp.maximum(block_position - 1, 1))
    second_pick = second_pick + (second_pick >= first_pick).astype(jnp.int32)
    second_pick = jnp.where(block_position >= 2, second_pick, 0)
    return jnp.stack([first_pick, second_pick], axis=1).astype(jnp.int32)


def shard_levels(key, extent, split, low, high):
    def one(dim, shards_of):
        draws = jax.random.uniform(jax.random.fold_in(jax.random.fold_in(key, 6), dim), (shards_of,), jnp.float32, low / len(split), high / len(split))
        return jnp.repeat(jnp.exp(draws), extent[dim] // shards_of).reshape((-1,) + (1,) * (len(extent) - dim - 1))

    factor_of = one(*split[0])
    for cut in split[1:]:
        factor_of = factor_of * one(*cut)
    return factor_of


def scatter_about(key, dims, width, bound, shards=(), kind=jnp.bfloat16):
    drawn = jax.random.normal(key, dims, jnp.float32) * width
    if len(shards) > 0:
        drawn = shard_levels(key, dims, shards, -0.22, 0.18) * drawn
    return jnp.clip(drawn, min=-bound, max=bound).astype(kind)


def setup_inputs(seed: int = 0, part: int = 0) -> dict:
    keys = jax.random.split(jax.random.key(seed), 5)
    part_splits = jax.random.split(jax.random.fold_in(keys[4], part), 5)
    queries = draw_queries(jax.random.fold_in(jax.random.fold_in(keys[4], part), 71), part)
    all_key_states = draw_all_key_states(jax.random.fold_in(jax.random.fold_in(keys[4], part), 71), part)
    all_value_states = scatter_about(part_splits[2], (CONTEXT_TOKENS, KEY_VALUE_HEADS * HEAD_SIZE), 1.0, 6.0, ((0, 16),))
    selected = draw_selected(jax.random.fold_in(jax.random.fold_in(keys[4], part), 71), part)
    return dict(queries=queries, all_key_states=all_key_states, all_value_states=all_value_states, selected=selected)


def reference(queries, all_key_states, all_value_states, selected):
    group_width = QUERY_HEADS // KEY_VALUE_HEADS
    score_scale = 1.0 / math.sqrt(HEAD_SIZE)
    row_ids = jnp.arange(BLOCK_TOKENS, dtype=jnp.int32)
    causal = row_ids[None, :] <= row_ids[:, None]

    def rows_for_block(source, block_number):
        return lax.dynamic_slice_in_dim(source, (block_number * BLOCK_TOKENS).astype(jnp.int32), BLOCK_TOKENS, 0)

    def one_block(block_position):
        first_block = selected[block_position, 0]
        second_block = selected[block_position, 1]
        first_valid = first_block < block_position
        second_valid = jnp.logical_and(second_block < block_position, second_block != first_block)
        query_row_block = rows_for_block(queries, block_position).astype(jnp.float32).reshape(BLOCK_TOKENS, KEY_VALUE_HEADS, group_width, HEAD_SIZE)
        key_row_block = jnp.concatenate([rows_for_block(all_key_states, block_position), rows_for_block(all_key_states, first_block), rows_for_block(all_key_states, second_block)], axis=0)
        value_row_block = jnp.concatenate([rows_for_block(all_value_states, block_position), rows_for_block(all_value_states, first_block), rows_for_block(all_value_states, second_block)], axis=0)
        key_row_block = key_row_block.astype(jnp.float32).reshape(3 * BLOCK_TOKENS, KEY_VALUE_HEADS, HEAD_SIZE)
        value_row_block = value_row_block.astype(jnp.float32).reshape(3 * BLOCK_TOKENS, KEY_VALUE_HEADS, HEAD_SIZE)
        allowed = jnp.concatenate([causal, jnp.broadcast_to(first_valid, (BLOCK_TOKENS, BLOCK_TOKENS)), jnp.broadcast_to(second_valid, (BLOCK_TOKENS, BLOCK_TOKENS))], axis=1)
        scores = jnp.einsum('tgrd,ugd->tgru', query_row_block, key_row_block) * score_scale
        scores = jnp.where(allowed[:, None, None, :], scores, jnp.float32(-1e+30))
        row_max = lax.optimization_barrier(jnp.max(scores, axis=3, keepdims=True))
        weights = jnp.exp(scores - row_max)
        row_sum = lax.optimization_barrier(jnp.sum(weights, axis=3, keepdims=True))
        rounded = lax.optimization_barrier(weights.astype(jnp.bfloat16)).astype(jnp.float32)
        mixture = jnp.einsum('tgru,ugd->tgrd', rounded, value_row_block)
        return (mixture / row_sum).astype(jnp.bfloat16).reshape(BLOCK_TOKENS, QUERY_HEADS * HEAD_SIZE)
    result = lax.map(one_block, jnp.arange(NBLK, dtype=jnp.int32))
    return result.reshape(CONTEXT_TOKENS, QUERY_HEADS * HEAD_SIZE)
```

```python
import functools
import math

import jax
import jax.numpy as jnp
from jax import lax
from jax.experimental import pallas as pl
from jax.experimental.pallas import tpu as pltpu
from jax.sharding import PartitionSpec as P

QUERY_HEADS = 32
KEY_VALUE_HEADS = 4
HEAD_SIZE = 128
GROUP_WIDTH = QUERY_HEADS // KEY_VALUE_HEADS
EXPONENT_SCALE = math.log2(math.e) / math.sqrt(HEAD_SIZE)
MASKED = -1e30
LAYERS = 4
SIDE = 4
MESH = pl.DeviceIdType.MESH


def attend_head(queries, keys, values, causal, first_valid, second_valid, rows):
    scores = lax.dot_general(
        queries, keys, (((1,), (1,)), ((), ())), preferred_element_type=jnp.float32
    )
    own = jnp.where(causal, scores[:, :rows], MASKED)
    first = scores[:, rows : 2 * rows]
    second = scores[:, 2 * rows :]
    own_max = jnp.max(own, axis=1, keepdims=True)
    first_max = jnp.where(first_valid, jnp.max(first, axis=1, keepdims=True), MASKED)
    second_max = jnp.where(second_valid, jnp.max(second, axis=1, keepdims=True), MASKED)
    row_max = jnp.maximum(own_max, jnp.maximum(first_max, second_max))
    own = jnp.exp2((own - row_max) * EXPONENT_SCALE)
    first = jnp.exp2((first - jnp.where(first_valid, row_max, -MASKED)) * EXPONENT_SCALE)
    second = jnp.exp2((second - jnp.where(second_valid, row_max, -MASKED)) * EXPONENT_SCALE)
    row_sum = jnp.sum(own + first + second, axis=1, keepdims=True)
    weights = jnp.concatenate(
        [own.astype(jnp.bfloat16), first.astype(jnp.bfloat16), second.astype(jnp.bfloat16)], axis=1
    )
    mixture = jnp.dot(weights, values, preferred_element_type=jnp.float32)
    return (mixture * (1.0 / row_sum)).astype(jnp.bfloat16)


def relay_kernel(
    rows,
    selected_ref,
    query_ref,
    key_ref,
    value_ref,
    out_ref,
    *scratch,
):
    heads = KEY_VALUE_HEADS
    stores = scratch[:heads]
    gathered = scratch[heads : 2 * heads]
    upward = scratch[2 * heads : 3 * heads]
    outgoing = scratch[3 * heads : 4 * heads]
    (
        request_vmem,
        request_smem,
        request_send,
        request_recv,
        spread_send,
        spread_recv,
        chain_send,
        chain_recv,
        deliver_send,
        deliver_recv,
        local_sem,
    ) = scratch[4 * heads :]
    quarter = rows // SIDE
    me = lax.axis_index("ctx")
    layer = me // SIDE
    place = me % SIDE

    def peer(offset):
        return layer * SIDE + (place + offset) % SIDE

    for g in range(heads):
        columns = slice(g * HEAD_SIZE, (g + 1) * HEAD_SIZE)
        gathered[g][0, 0] = key_ref[:, columns]
        gathered[g][1, 0] = value_ref[:, columns]
    lane = lax.broadcasted_iota(jnp.int32, (1, 128), 1)
    request_vmem[place] = jnp.where(lane == 0, selected_ref[0, 0], selected_ref[0, 1])

    barrier = pltpu.get_barrier_semaphore()
    for offset in range(1, SIDE):
        pl.semaphore_signal(barrier, inc=1, device_id={"ctx": peer(offset)}, device_id_type=MESH)

    @pl.when(layer > 0)
    def _():
        for q in range(SIDE):
            pl.semaphore_signal(
                barrier, inc=1, device_id={"ctx": (layer - 1) * SIDE + q}, device_id_type=MESH
            )

    @pl.when(layer < LAYERS - 1)
    def _():
        for q in range(SIDE):
            pl.semaphore_signal(
                barrier, inc=1, device_id={"ctx": (layer + 1) * SIDE + q}, device_id_type=MESH
            )

    neighbour_layers = jnp.minimum(layer, 1) + jnp.minimum(LAYERS - 1 - layer, 1)
    pl.semaphore_wait(barrier, SIDE - 1 + SIDE * neighbour_layers)

    def spread(g, offset):
        target = (place + offset) % SIDE
        return pltpu.make_async_remote_copy(
            src_ref=gathered[g].at[:, 0, pl.ds(target * quarter, quarter), :],
            dst_ref=stores[g].at[me],
            send_sem=spread_send.at[g, offset - 1],
            recv_sem=spread_recv.at[g, offset - 1],
            device_id={"ctx": peer(offset)},
            device_id_type=MESH,
        )

    def request(offset):
        return pltpu.make_async_remote_copy(
            src_ref=request_vmem.at[place],
            dst_ref=request_vmem.at[place],
            send_sem=request_send.at[offset - 1],
            recv_sem=request_recv.at[offset - 1],
            device_id={"ctx": peer(offset)},
            device_id_type=MESH,
        )

    def request_down(offset):
        return pltpu.make_async_remote_copy(
            src_ref=request_vmem.at[place],
            dst_ref=request_vmem.at[SIDE + place],
            send_sem=request_send.at[SIDE - 1 + offset],
            recv_sem=request_recv.at[SIDE - 1 + offset],
            device_id={"ctx": (LAYERS - 2) * SIDE + (place + offset) % SIDE},
            device_id_type=MESH,
        )

    def chain(g, source_layer, slot):
        part = stores[g].at[pl.ds(source_layer * SIDE, SIDE)]
        return pltpu.make_async_remote_copy(
            src_ref=part,
            dst_ref=part,
            send_sem=chain_send.at[g, slot],
            recv_sem=chain_recv.at[g, slot],
            device_id={"ctx": (layer + 1) % LAYERS * SIDE + place},
            device_id_type=MESH,
        )

    def chain_top(g):
        return pltpu.make_async_remote_copy(
            src_ref=upward[g].at[pl.ds(0, 2 * SIDE - 1)],
            dst_ref=stores[g].at[pl.ds(0, 2 * SIDE - 1)],
            send_sem=chain_send.at[g, 0],
            recv_sem=chain_recv.at[g, 0],
            device_id={"ctx": (LAYERS - 1) * SIDE + place},
            device_id_type=MESH,
        )

    def deliver(g, offset):
        return pltpu.make_async_remote_copy(
            src_ref=outgoing[g].at[offset - 1],
            dst_ref=gathered[g].at[:, pl.ds(1, 2), pl.ds(place * quarter, quarter), :],
            send_sem=deliver_send.at[g, offset - 1],
            recv_sem=deliver_recv.at[g, offset - 1],
            device_id={"ctx": peer(offset)},
            device_id_type=MESH,
        )

    for offset in range(1, SIDE):
        request(offset).start()

    @pl.when(layer == LAYERS - 1)
    def _():
        for offset in range(SIDE):
            request_down(offset).start()

    for g in range(heads):
        for offset in range(1, SIDE):
            spread(g, offset).start()
        stores[g][me] = gathered[g][:, 0, pl.ds(place * quarter, quarter), :]

    for offset in range(1, SIDE):
        request(offset).wait_recv()

    @pl.when(layer == LAYERS - 2)
    def _():
        for offset in range(SIDE):
            request_down(offset).wait_recv()

    @pl.when(layer != LAYERS - 2)
    def _():
        for q in range(SIDE):
            request_vmem[SIDE + q] = jnp.zeros((1, 128), jnp.int32)

    to_smem = pltpu.make_async_copy(request_vmem, request_smem, local_sem)
    to_smem.start()
    to_smem.wait()

    first_valid = selected_ref[0, 0] < me
    second_valid = jnp.logical_and(
        selected_ref[0, 1] < me, selected_ref[0, 1] != selected_ref[0, 0]
    )
    causal = lax.broadcasted_iota(jnp.int32, (rows, rows), 1) <= lax.broadcasted_iota(
        jnp.int32, (rows, rows), 0
    )

    def wait_spread(g):
        for offset in range(1, SIDE):
            spread(g, offset).wait_recv()

    def pass_on(g):
        @pl.when(layer == 0)
        def _():
            chain(g, 0, 0).start()

        @pl.when(layer == 1)
        def _():
            chain(g, 1, 0).start()
            chain(g, 0, 0).wait_recv()
            chain(g, 0, 1).start()

        @pl.when(layer == 2)
        def _():
            chain(g, 1, 0).wait_recv()
            chain(g, 0, 1).wait_recv()
            for slot in range(2 * SIDE - 1):
                wanted = request_smem[SIDE + slot % SIDE, 0, 1 - slot // SIDE]
                upward[g][slot] = stores[g][jnp.minimum(wanted, (LAYERS - 1) * SIDE - 1)]
            chain_top(g).start()

        @pl.when(layer == LAYERS - 1)
        def _():
            chain_top(g).wait_recv()

    def hand_out(g):
        def wanted_piece(q, choice):
            wanted = request_smem[q, 0, choice]
            top = jnp.logical_and(layer == LAYERS - 1, wanted < (LAYERS - 1) * SIDE)
            return stores[g][jnp.where(top, q + SIDE * (1 - choice), wanted)]

        for offset in range(1, SIDE):
            for choice in range(2):
                piece = wanted_piece((place + offset) % SIDE, choice)
                outgoing[g][offset - 1, :, choice] = piece
            deliver(g, offset).start()
        for choice in range(2):
            gathered[g][:, 1 + choice, pl.ds(place * quarter, quarter), :] = wanted_piece(
                place, choice
            )

    def compute(g):
        for offset in range(1, SIDE):
            deliver(g, offset).wait_recv()

        def head(index, carry):
            column = pl.multiple_of((g * GROUP_WIDTH + index) * HEAD_SIZE, HEAD_SIZE)
            out_ref[:, pl.ds(column, HEAD_SIZE)] = attend_head(
                query_ref[:, pl.ds(column, HEAD_SIZE)],
                gathered[g][0].reshape(3 * rows, HEAD_SIZE),
                gathered[g][1].reshape(3 * rows, HEAD_SIZE),
                causal,
                first_valid,
                second_valid,
                rows,
            )
            return carry

        lax.fori_loop(0, GROUP_WIDTH, head, 0)

    for g in range(heads):
        wait_spread(g)
        pass_on(g)
        hand_out(g)
        if g > 0:
            compute(g - 1)
    compute(heads - 1)

    for offset in range(1, SIDE):
        request(offset).wait_send()

    @pl.when(layer == LAYERS - 1)
    def _():
        for offset in range(SIDE):
            request_down(offset).wait_send()

    for g in range(heads):
        for offset in range(1, SIDE):
            spread(g, offset).wait_send()
            deliver(g, offset).wait_send()

        @pl.when(layer == 0)
        def _():
            chain(g, 0, 0).wait_send()

        @pl.when(layer == 1)
        def _():
            chain(g, 1, 0).wait_send()
            chain(g, 0, 1).wait_send()

        @pl.when(layer == 2)
        def _():
            chain_top(g).wait_send()


def relayed(queries, all_key_states, all_value_states, selected):
    rows = queries.shape[0]
    quarter = rows // SIDE
    heads = KEY_VALUE_HEADS
    blocks = LAYERS * SIDE
    kind = all_key_states.dtype
    vmem = pl.BlockSpec(memory_space=pltpu.VMEM)
    dma = pltpu.SemaphoreType.DMA
    return pl.pallas_call(
        functools.partial(relay_kernel, rows),
        out_shape=jax.ShapeDtypeStruct(queries.shape, queries.dtype),
        in_specs=[pl.BlockSpec(memory_space=pltpu.SMEM), vmem, vmem, vmem],
        out_specs=vmem,
        scratch_shapes=[pltpu.VMEM((blocks, 2, quarter, HEAD_SIZE), kind)] * heads
        + [pltpu.VMEM((2, 3, rows, HEAD_SIZE), kind)] * heads
        + [pltpu.VMEM((2 * SIDE, 2, quarter, HEAD_SIZE), kind)] * heads
        + [pltpu.VMEM((SIDE - 1, 2, 2, quarter, HEAD_SIZE), kind)] * heads
        + [
            pltpu.VMEM((2 * SIDE, 1, 128), jnp.int32),
            pltpu.SMEM((2 * SIDE, 1, 128), jnp.int32),
            dma((2 * SIDE - 1,)),
            dma((2 * SIDE - 1,)),
            dma((heads, SIDE - 1)),
            dma((heads, SIDE - 1)),
            dma((heads, 2)),
            dma((heads, 2)),
            dma((heads, SIDE - 1)),
            dma((heads, SIDE - 1)),
            dma,
        ],
        compiler_params=pltpu.CompilerParams(
            collective_id=0, has_side_effects=True, vmem_limit_bytes=40 * 2**20
        ),
    )(selected, queries, all_key_states, all_value_states)


def attend_kernel(valid_ref, query_ref, key_ref, value_ref, out_ref):
    rows = query_ref.shape[0]
    causal = lax.broadcasted_iota(jnp.int32, (rows, rows), 1) <= lax.broadcasted_iota(
        jnp.int32, (rows, rows), 0
    )
    out_ref[...] = attend_head(
        query_ref[...],
        key_ref[...],
        value_ref[...],
        causal,
        valid_ref[0] != 0,
        valid_ref[1] != 0,
        rows,
    )


def exchanged(queries, all_key_states, all_value_states, selected):
    devices = lax.axis_size("ctx")
    me = lax.axis_index("ctx")
    rows, width = all_key_states.shape
    exchange = functools.partial(
        lax.all_to_all, axis_name="ctx", split_axis=0, concat_axis=0, tiled=True
    )
    both = jnp.concatenate([all_key_states, all_value_states], axis=1)
    requests = lax.all_gather(selected, "ctx", axis=0, tiled=True)
    held = exchange(both.reshape(devices, rows // devices, 2 * width))
    chosen = [
        exchange(jnp.take(held, requests[:, choice], axis=0)).reshape(rows, 2 * width)
        for choice in range(2)
    ]
    everything = jnp.concatenate([both] + chosen, axis=0)
    first, second = selected[0, 0], selected[0, 1]
    valid = jnp.stack([first < me, jnp.logical_and(second < me, second != first)])
    return pl.pallas_call(
        attend_kernel,
        out_shape=jax.ShapeDtypeStruct(queries.shape, queries.dtype),
        grid=(QUERY_HEADS,),
        in_specs=[
            pl.BlockSpec(memory_space=pltpu.SMEM),
            pl.BlockSpec((rows, HEAD_SIZE), lambda h: (0, h)),
            pl.BlockSpec((3 * rows, HEAD_SIZE), lambda h: (0, h // GROUP_WIDTH)),
            pl.BlockSpec((3 * rows, HEAD_SIZE), lambda h: (0, KEY_VALUE_HEADS + h // GROUP_WIDTH)),
        ],
        out_specs=pl.BlockSpec((rows, HEAD_SIZE), lambda h: (0, h)),
    )(valid.astype(jnp.int32), queries, everything, everything)


def solution(mesh):
    placed = P(("groups", "ctx"), None)
    local = relayed if mesh.shape["ctx"] == LAYERS * SIDE else exchanged
    return jax.shard_map(
        local, mesh=mesh, in_specs=(placed,) * 4, out_specs=placed, check_vma=False
    )
```

```python
import functools
import math

import jax
import jax.numpy as jnp
from jax import lax
from jax.experimental import pallas as pl
from jax.experimental.pallas import tpu as pltpu
from jax.sharding import PartitionSpec as P

QUERY_HEADS = 32
KEY_VALUE_HEADS = 4
HEAD_SIZE = 128
GROUP_WIDTH = QUERY_HEADS // KEY_VALUE_HEADS
EXPONENT_SCALE = math.log2(math.e) / math.sqrt(HEAD_SIZE)
MASKED = -1e30
LAYERS = 4
SIDE = 4
MESH = pl.DeviceIdType.MESH


def half_max(scores):
    return jnp.maximum(scores[:, :HEAD_SIZE], scores[:, HEAD_SIZE:])


def attend_head(queries, keys, values, causal, first_valid, second_valid):
    rows = queries.shape[0]
    scores = lax.dot_general(
        queries, keys, (((1,), (1,)), ((), ())), preferred_element_type=jnp.float32
    )
    own = jnp.where(causal, scores[:, :rows], MASKED)
    first = scores[:, rows : 2 * rows]
    second = scores[:, 2 * rows :]
    row_max = jnp.max(
        jnp.maximum(
            half_max(own),
            jnp.maximum(
                jnp.where(first_valid, half_max(first), MASKED),
                jnp.where(second_valid, half_max(second), MASKED),
            ),
        ),
        axis=1,
        keepdims=True,
    )
    first_max = jnp.where(first_valid, row_max, -MASKED)
    second_max = jnp.where(second_valid, row_max, -MASKED)
    weights = jnp.concatenate(
        [
            jnp.exp2((part - top) * EXPONENT_SCALE).astype(jnp.bfloat16)
            for part, top in ((own, row_max), (first, first_max), (second, second_max))
        ],
        axis=1,
    )
    mixture = jnp.dot(weights, values, preferred_element_type=jnp.float32)
    return (mixture[:, :HEAD_SIZE] * (1.0 / mixture[:, HEAD_SIZE:])).astype(jnp.bfloat16)


def with_ones(values):
    return jnp.concatenate([values, jnp.ones_like(values)], axis=1)


def relay_kernel(
    rows,
    selected_hbm,
    query_hbm,
    key_hbm,
    value_hbm,
    out_ref,
    *scratch,
):
    heads = KEY_VALUE_HEADS
    stores = scratch[:heads]
    gathered = scratch[heads : 2 * heads]
    upward = scratch[2 * heads : 3 * heads]
    outgoing = scratch[3 * heads : 4 * heads]
    (
        request_vmem,
        request_smem,
        request_send,
        request_recv,
        spread_send,
        spread_recv,
        chain_send,
        chain_recv,
        deliver_send,
        deliver_recv,
        local_sem,
        selected_ref,
        query_ref,
        selected_sem,
        query_sem,
        pack_sem,
    ) = scratch[4 * heads :]
    quarter = rows // SIDE
    me = lax.axis_index("ctx")
    layer = me // SIDE
    place = me % SIDE

    def peer(offset):
        return layer * SIDE + (place + offset) % SIDE

    def pack(g, which):
        source = (key_hbm, value_hbm)[which]
        return pltpu.make_async_copy(
            source.at[:, pl.ds(g * HEAD_SIZE, HEAD_SIZE)],
            gathered[g].at[which, 0],
            pack_sem.at[g, which],
        )

    def fetch_queries(g):
        columns = pl.ds(g * GROUP_WIDTH * HEAD_SIZE, GROUP_WIDTH * HEAD_SIZE)
        return pltpu.make_async_copy(
            query_hbm.at[:, columns], query_ref.at[:, columns], query_sem.at[g]
        )

    fetch_selected = pltpu.make_async_copy(selected_hbm, selected_ref, selected_sem)
    fetch_selected.start()
    for g in range(heads):
        for which in range(2):
            pack(g, which).start()
    for g in range(heads):
        fetch_queries(g).start()

    barrier = pltpu.get_barrier_semaphore()
    for offset in range(1, SIDE):
        pl.semaphore_signal(barrier, inc=1, device_id={"ctx": peer(offset)}, device_id_type=MESH)

    @pl.when(layer > 0)
    def _():
        for q in range(SIDE):
            pl.semaphore_signal(
                barrier, inc=1, device_id={"ctx": (layer - 1) * SIDE + q}, device_id_type=MESH
            )

    @pl.when(layer < LAYERS - 1)
    def _():
        for q in range(SIDE):
            pl.semaphore_signal(
                barrier, inc=1, device_id={"ctx": (layer + 1) * SIDE + q}, device_id_type=MESH
            )

    neighbour_layers = jnp.minimum(layer, 1) + jnp.minimum(LAYERS - 1 - layer, 1)
    pl.semaphore_wait(barrier, SIDE - 1 + SIDE * neighbour_layers)

    fetch_selected.wait()
    lane = lax.broadcasted_iota(jnp.int32, (1, 128), 1)
    request_vmem[place] = jnp.where(lane == 0, selected_ref[0, 0], selected_ref[0, 1])

    def spread(g, offset):
        target = (place + offset) % SIDE
        return pltpu.make_async_remote_copy(
            src_ref=gathered[g].at[:, 0, pl.ds(target * quarter, quarter), :],
            dst_ref=stores[g].at[me],
            send_sem=spread_send.at[g, offset - 1],
            recv_sem=spread_recv.at[g, offset - 1],
            device_id={"ctx": peer(offset)},
            device_id_type=MESH,
        )

    def request(offset):
        return pltpu.make_async_remote_copy(
            src_ref=request_vmem.at[place],
            dst_ref=request_vmem.at[place],
            send_sem=request_send.at[offset - 1],
            recv_sem=request_recv.at[offset - 1],
            device_id={"ctx": peer(offset)},
            device_id_type=MESH,
        )

    def request_down(offset):
        return pltpu.make_async_remote_copy(
            src_ref=request_vmem.at[place],
            dst_ref=request_vmem.at[SIDE + place],
            send_sem=request_send.at[SIDE - 1 + offset],
            recv_sem=request_recv.at[SIDE - 1 + offset],
            device_id={"ctx": (LAYERS - 2) * SIDE + (place + offset) % SIDE},
            device_id_type=MESH,
        )

    def chain(g, source_layer, slot):
        part = stores[g].at[pl.ds(source_layer * SIDE, SIDE)]
        return pltpu.make_async_remote_copy(
            src_ref=part,
            dst_ref=part,
            send_sem=chain_send.at[g, slot],
            recv_sem=chain_recv.at[g, slot],
            device_id={"ctx": (layer + 1) % LAYERS * SIDE + place},
            device_id_type=MESH,
        )

    def chain_top(g):
        return pltpu.make_async_remote_copy(
            src_ref=upward[g].at[pl.ds(0, 2 * SIDE - 1)],
            dst_ref=stores[g].at[pl.ds(0, 2 * SIDE - 1)],
            send_sem=chain_send.at[g, 0],
            recv_sem=chain_recv.at[g, 0],
            device_id={"ctx": (LAYERS - 1) * SIDE + place},
            device_id_type=MESH,
        )

    def deliver(g, offset):
        return pltpu.make_async_remote_copy(
            src_ref=outgoing[g].at[offset - 1],
            dst_ref=gathered[g].at[:, pl.ds(1, 2), pl.ds(place * quarter, quarter), :],
            send_sem=deliver_send.at[g, offset - 1],
            recv_sem=deliver_recv.at[g, offset - 1],
            device_id={"ctx": peer(offset)},
            device_id_type=MESH,
        )

    for offset in range(1, SIDE):
        request(offset).start()

    @pl.when(layer == LAYERS - 1)
    def _():
        for offset in range(SIDE):
            request_down(offset).start()

    for g in range(heads):
        for which in range(2):
            pack(g, which).wait()
        for offset in range(1, SIDE):
            spread(g, offset).start()
        stores[g][me] = gathered[g][:, 0, pl.ds(place * quarter, quarter), :]

    for offset in range(1, SIDE):
        request(offset).wait_recv()

    @pl.when(layer == LAYERS - 2)
    def _():
        for offset in range(SIDE):
            request_down(offset).wait_recv()

    @pl.when(layer != LAYERS - 2)
    def _():
        for q in range(SIDE):
            request_vmem[SIDE + q] = jnp.zeros((1, 128), jnp.int32)

    to_smem = pltpu.make_async_copy(request_vmem, request_smem, local_sem)
    to_smem.start()
    to_smem.wait()

    first_valid = selected_ref[0, 0] < me
    second_valid = jnp.logical_and(
        selected_ref[0, 1] < me, selected_ref[0, 1] != selected_ref[0, 0]
    )
    causal = lax.broadcasted_iota(jnp.int32, (rows, rows), 1) <= lax.broadcasted_iota(
        jnp.int32, (rows, rows), 0
    )

    def wait_spread(g):
        for offset in range(1, SIDE):
            spread(g, offset).wait_recv()

    def pass_on_low(g):
        @pl.when(layer == 0)
        def _():
            chain(g, 0, 0).start()

        @pl.when(layer == 1)
        def _():
            chain(g, 1, 0).start()
            chain(g, 0, 0).wait_recv()
            chain(g, 0, 1).start()

    def pass_on_high(g):
        @pl.when(layer == 2)
        def _():
            chain(g, 1, 0).wait_recv()
            chain(g, 0, 1).wait_recv()
            for slot in range(2 * SIDE - 1):
                wanted = request_smem[SIDE + slot % SIDE, 0, 1 - slot // SIDE]
                upward[g][slot] = stores[g][jnp.minimum(wanted, (LAYERS - 1) * SIDE - 1)]
            chain_top(g).start()

        @pl.when(layer == LAYERS - 1)
        def _():
            chain_top(g).wait_recv()

    def hand_out(g):
        def wanted_piece(q, choice):
            wanted = request_smem[q, 0, choice]
            top = jnp.logical_and(layer == LAYERS - 1, wanted < (LAYERS - 1) * SIDE)
            return stores[g][jnp.where(top, q + SIDE * (1 - choice), wanted)]

        for offset in range(1, SIDE):
            for choice in range(2):
                piece = wanted_piece((place + offset) % SIDE, choice)
                outgoing[g][offset - 1, :, choice] = piece
            deliver(g, offset).start()
        for choice in range(2):
            gathered[g][:, 1 + choice, pl.ds(place * quarter, quarter), :] = wanted_piece(
                place, choice
            )

    def compute(g):
        for offset in range(1, SIDE):
            deliver(g, offset).wait_recv()

        fetch_queries(g).wait()
        keys = gathered[g][0].reshape(3 * rows, HEAD_SIZE)
        values = with_ones(gathered[g][1].reshape(3 * rows, HEAD_SIZE))
        for index in range(GROUP_WIDTH):
            columns = pl.ds((g * GROUP_WIDTH + index) * HEAD_SIZE, HEAD_SIZE)
            out_ref[:, columns] = attend_head(
                query_ref[:, columns], keys, values, causal, first_valid, second_valid
            )

    @pl.when(layer < LAYERS - 2)
    def _():
        for g in range(heads):
            wait_spread(g)
            pass_on_low(g)

    for g in range(heads):

        @pl.when(layer >= LAYERS - 2)
        def _():
            wait_spread(g)
            pass_on_high(g)

        hand_out(g)
        if g > 0:
            compute(g - 1)
    compute(heads - 1)

    for offset in range(1, SIDE):
        request(offset).wait_send()

    @pl.when(layer == LAYERS - 1)
    def _():
        for offset in range(SIDE):
            request_down(offset).wait_send()

    for g in range(heads):
        for offset in range(1, SIDE):
            spread(g, offset).wait_send()
            deliver(g, offset).wait_send()

        @pl.when(layer == 0)
        def _():
            chain(g, 0, 0).wait_send()

        @pl.when(layer == 1)
        def _():
            chain(g, 1, 0).wait_send()
            chain(g, 0, 1).wait_send()

        @pl.when(layer == 2)
        def _():
            chain_top(g).wait_send()


def relayed(queries, all_key_states, all_value_states, selected):
    rows = queries.shape[0]
    quarter = rows // SIDE
    heads = KEY_VALUE_HEADS
    blocks = LAYERS * SIDE
    kind = all_key_states.dtype
    vmem = pl.BlockSpec(memory_space=pltpu.VMEM)
    dma = pltpu.SemaphoreType.DMA
    return pl.pallas_call(
        functools.partial(relay_kernel, rows),
        out_shape=jax.ShapeDtypeStruct(queries.shape, queries.dtype),
        in_specs=[pl.BlockSpec(memory_space=pl.ANY)] * 4,
        out_specs=vmem,
        scratch_shapes=[pltpu.VMEM((blocks, 2, quarter, HEAD_SIZE), kind)] * heads
        + [pltpu.VMEM((2, 3, rows, HEAD_SIZE), kind)] * heads
        + [pltpu.VMEM((2 * SIDE, 2, quarter, HEAD_SIZE), kind)] * heads
        + [pltpu.VMEM((SIDE - 1, 2, 2, quarter, HEAD_SIZE), kind)] * heads
        + [
            pltpu.VMEM((2 * SIDE, 1, 128), jnp.int32),
            pltpu.SMEM((2 * SIDE, 1, 128), jnp.int32),
            dma((2 * SIDE - 1,)),
            dma((2 * SIDE - 1,)),
            dma((heads, SIDE - 1)),
            dma((heads, SIDE - 1)),
            dma((heads, 2)),
            dma((heads, 2)),
            dma((heads, SIDE - 1)),
            dma((heads, SIDE - 1)),
            dma,
            pltpu.SMEM((1, 2), jnp.int32),
            pltpu.VMEM(queries.shape, queries.dtype),
            dma,
            dma((heads,)),
            dma((heads, 2)),
        ],
        compiler_params=pltpu.CompilerParams(
            collective_id=0, has_side_effects=True, vmem_limit_bytes=60 * 2**20
        ),
    )(selected, queries, all_key_states, all_value_states)


def attend_kernel(valid_ref, query_ref, key_ref, value_ref, out_ref):
    rows = query_ref.shape[0]
    causal = lax.broadcasted_iota(jnp.int32, (rows, rows), 1) <= lax.broadcasted_iota(
        jnp.int32, (rows, rows), 0
    )
    out_ref[...] = attend_head(
        query_ref[...],
        key_ref[...],
        with_ones(value_ref[...]),
        causal,
        valid_ref[0] != 0,
        valid_ref[1] != 0,
    )


def exchanged(queries, all_key_states, all_value_states, selected):
    devices = lax.axis_size("ctx")
    me = lax.axis_index("ctx")
    rows, width = all_key_states.shape
    exchange = functools.partial(
        lax.all_to_all, axis_name="ctx", split_axis=0, concat_axis=0, tiled=True
    )
    both = jnp.concatenate([all_key_states, all_value_states], axis=1)
    requests = lax.all_gather(selected, "ctx", axis=0, tiled=True)
    held = exchange(both.reshape(devices, rows // devices, 2 * width))
    chosen = [
        exchange(jnp.take(held, requests[:, choice], axis=0)).reshape(rows, 2 * width)
        for choice in range(2)
    ]
    everything = jnp.concatenate([both] + chosen, axis=0)
    first, second = selected[0, 0], selected[0, 1]
    valid = jnp.stack([first < me, jnp.logical_and(second < me, second != first)])
    return pl.pallas_call(
        attend_kernel,
        out_shape=jax.ShapeDtypeStruct(queries.shape, queries.dtype),
        grid=(QUERY_HEADS,),
        in_specs=[
            pl.BlockSpec(memory_space=pltpu.SMEM),
            pl.BlockSpec((rows, HEAD_SIZE), lambda h: (0, h)),
            pl.BlockSpec((3 * rows, HEAD_SIZE), lambda h: (0, h // GROUP_WIDTH)),
            pl.BlockSpec((3 * rows, HEAD_SIZE), lambda h: (0, KEY_VALUE_HEADS + h // GROUP_WIDTH)),
        ],
        out_specs=pl.BlockSpec((rows, HEAD_SIZE), lambda h: (0, h)),
    )(valid.astype(jnp.int32), queries, everything, everything)


def solution(mesh):
    placed = P(("groups", "ctx"), None)
    local = relayed if mesh.shape["ctx"] == LAYERS * SIDE else exchanged
    return jax.shard_map(
        local, mesh=mesh, in_specs=(placed,) * 4, out_specs=placed, check_vma=False
    )
```

```python
import functools
import math

import jax
import jax.numpy as jnp
from jax import lax
from jax.experimental import pallas as pl
from jax.experimental.pallas import tpu as pltpu
from jax.sharding import PartitionSpec as P

QUERY_HEADS = 32
KEY_VALUE_HEADS = 4
HEAD_SIZE = 128
GROUP_WIDTH = QUERY_HEADS // KEY_VALUE_HEADS
EXPONENT_SCALE = math.log2(math.e) / math.sqrt(HEAD_SIZE)
MASKED = -1e30
LAYERS = 4
SIDE = 4
MESH = pl.DeviceIdType.MESH


def half_max(scores):
    return jnp.maximum(scores[:, :HEAD_SIZE], scores[:, HEAD_SIZE:])


def attend_head(queries, keys, values, causal, first_valid, second_valid):
    rows = queries.shape[0]
    scores = lax.dot_general(
        queries, keys, (((1,), (1,)), ((), ())), preferred_element_type=jnp.float32
    )
    own = jnp.where(causal, scores[:, :rows], MASKED)
    first = scores[:, rows : 2 * rows]
    second = scores[:, 2 * rows :]
    row_max = jnp.max(
        jnp.maximum(
            half_max(own),
            jnp.maximum(
                jnp.where(first_valid, half_max(first), MASKED),
                jnp.where(second_valid, half_max(second), MASKED),
            ),
        ),
        axis=1,
        keepdims=True,
    )
    first_max = jnp.where(first_valid, row_max, -MASKED)
    second_max = jnp.where(second_valid, row_max, -MASKED)
    weights = jnp.concatenate(
        [
            jnp.exp2((part - top) * EXPONENT_SCALE).astype(jnp.bfloat16)
            for part, top in ((own, row_max), (first, first_max), (second, second_max))
        ],
        axis=1,
    )
    mixture = jnp.dot(weights, values, preferred_element_type=jnp.float32)
    return (mixture[:, :HEAD_SIZE] * (1.0 / mixture[:, HEAD_SIZE:])).astype(jnp.bfloat16)


def with_ones(values):
    return jnp.concatenate([values, jnp.ones_like(values)], axis=1)


def relay_kernel(
    rows,
    selected_hbm,
    query_hbm,
    key_hbm,
    value_hbm,
    early_hbm,
    last_keys,
    last_values,
    *scratch,
):
    heads = KEY_VALUE_HEADS
    chunks = 2 * heads
    stores = scratch[:chunks]
    upward = scratch[chunks : 2 * chunks]
    outgoing = scratch[2 * chunks : 3 * chunks]
    gathered = scratch[3 * chunks : 4 * chunks - 2] + (last_keys, last_values)
    (
        request_vmem,
        request_smem,
        request_send,
        request_recv,
        spread_send,
        spread_recv,
        chain_send,
        chain_recv,
        deliver_send,
        deliver_recv,
        local_sem,
        selected_ref,
        query_ref,
        selected_sem,
        query_sem,
        pack_sem,
        early_ref,
        early_sem,
    ) = scratch[4 * chunks - 2 :]
    quarter = rows // SIDE
    me = lax.axis_index("ctx")
    layer = me // SIDE
    place = me % SIDE

    def peer(offset):
        return layer * SIDE + (place + offset) % SIDE

    def pack(c):
        source = (key_hbm, value_hbm)[c % 2]
        return pltpu.make_async_copy(
            source.at[:, pl.ds(c // 2 * HEAD_SIZE, HEAD_SIZE)],
            gathered[c].at[0],
            pack_sem.at[c],
        )

    def fetch_queries(g):
        columns = pl.ds(g * GROUP_WIDTH * HEAD_SIZE, GROUP_WIDTH * HEAD_SIZE)
        return pltpu.make_async_copy(
            query_hbm.at[:, columns], query_ref.at[:, columns], query_sem.at[g]
        )

    fetch_selected = pltpu.make_async_copy(selected_hbm, selected_ref, selected_sem)
    fetch_selected.start()
    for c in range(chunks):
        pack(c).start()
    for g in range(heads - 1):
        fetch_queries(g).start()

    barrier = pltpu.get_barrier_semaphore()
    for offset in range(1, SIDE):
        pl.semaphore_signal(barrier, inc=1, device_id={"ctx": peer(offset)}, device_id_type=MESH)

    @pl.when(layer > 0)
    def _():
        for q in range(SIDE):
            pl.semaphore_signal(
                barrier, inc=1, device_id={"ctx": (layer - 1) * SIDE + q}, device_id_type=MESH
            )

    @pl.when(layer < LAYERS - 1)
    def _():
        for q in range(SIDE):
            pl.semaphore_signal(
                barrier, inc=1, device_id={"ctx": (layer + 1) * SIDE + q}, device_id_type=MESH
            )

    neighbour_layers = jnp.minimum(layer, 1) + jnp.minimum(LAYERS - 1 - layer, 1)
    pl.semaphore_wait(barrier, SIDE - 1 + SIDE * neighbour_layers)

    fetch_selected.wait()
    lane = lax.broadcasted_iota(jnp.int32, (1, 128), 1)
    request_vmem[place] = jnp.where(lane == 0, selected_ref[0, 0], selected_ref[0, 1])

    def spread(g, offset):
        target = (place + offset) % SIDE
        return pltpu.make_async_remote_copy(
            src_ref=gathered[g].at[0, pl.ds(target * quarter, quarter), :],
            dst_ref=stores[g].at[me],
            send_sem=spread_send.at[g, offset - 1],
            recv_sem=spread_recv.at[g, offset - 1],
            device_id={"ctx": peer(offset)},
            device_id_type=MESH,
        )

    def request(offset):
        return pltpu.make_async_remote_copy(
            src_ref=request_vmem.at[place],
            dst_ref=request_vmem.at[place],
            send_sem=request_send.at[offset - 1],
            recv_sem=request_recv.at[offset - 1],
            device_id={"ctx": peer(offset)},
            device_id_type=MESH,
        )

    def request_down(offset):
        return pltpu.make_async_remote_copy(
            src_ref=request_vmem.at[place],
            dst_ref=request_vmem.at[SIDE + place],
            send_sem=request_send.at[SIDE - 1 + offset],
            recv_sem=request_recv.at[SIDE - 1 + offset],
            device_id={"ctx": (LAYERS - 2) * SIDE + (place + offset) % SIDE},
            device_id_type=MESH,
        )

    def chain(g, source_layer, slot):
        part = stores[g].at[pl.ds(source_layer * SIDE, SIDE)]
        return pltpu.make_async_remote_copy(
            src_ref=part,
            dst_ref=part,
            send_sem=chain_send.at[g, slot],
            recv_sem=chain_recv.at[g, slot],
            device_id={"ctx": (layer + 1) % LAYERS * SIDE + place},
            device_id_type=MESH,
        )

    def chain_top(g):
        return pltpu.make_async_remote_copy(
            src_ref=upward[g].at[pl.ds(0, 2 * SIDE - 1)],
            dst_ref=stores[g].at[pl.ds(0, 2 * SIDE - 1)],
            send_sem=chain_send.at[g, 0],
            recv_sem=chain_recv.at[g, 0],
            device_id={"ctx": (LAYERS - 1) * SIDE + place},
            device_id_type=MESH,
        )

    def deliver(g, offset):
        return pltpu.make_async_remote_copy(
            src_ref=outgoing[g].at[offset - 1],
            dst_ref=gathered[g].at[pl.ds(1, 2), pl.ds(place * quarter, quarter), :],
            send_sem=deliver_send.at[g, offset - 1],
            recv_sem=deliver_recv.at[g, offset - 1],
            device_id={"ctx": peer(offset)},
            device_id_type=MESH,
        )

    for offset in range(1, SIDE):
        request(offset).start()

    @pl.when(layer == LAYERS - 1)
    def _():
        for offset in range(SIDE):
            request_down(offset).start()

    for c in range(chunks):
        pack(c).wait()
        for offset in range(1, SIDE):
            spread(c, offset).start()
        stores[c][me] = gathered[c][0, pl.ds(place * quarter, quarter), :]

    for offset in range(1, SIDE):
        request(offset).wait_recv()

    @pl.when(layer == LAYERS - 2)
    def _():
        for offset in range(SIDE):
            request_down(offset).wait_recv()

    @pl.when(layer != LAYERS - 2)
    def _():
        for q in range(SIDE):
            request_vmem[SIDE + q] = jnp.zeros((1, 128), jnp.int32)

    to_smem = pltpu.make_async_copy(request_vmem, request_smem, local_sem)
    to_smem.start()
    to_smem.wait()

    first_valid = selected_ref[0, 0] < me
    second_valid = jnp.logical_and(
        selected_ref[0, 1] < me, selected_ref[0, 1] != selected_ref[0, 0]
    )
    causal = lax.broadcasted_iota(jnp.int32, (rows, rows), 1) <= lax.broadcasted_iota(
        jnp.int32, (rows, rows), 0
    )

    def wait_spread(g):
        for offset in range(1, SIDE):
            spread(g, offset).wait_recv()

    def pass_on_low(g):
        @pl.when(layer == 0)
        def _():
            chain(g, 0, 0).start()

        @pl.when(layer == 1)
        def _():
            if g == 0:
                chain(g, 1, 0).start()
            if g + 1 < chunks:
                wait_spread(g + 1)
                chain(g + 1, 1, 0).start()
            chain(g, 0, 0).wait_recv()
            chain(g, 0, 1).start()

    def pass_on_high(g):
        @pl.when(layer == 2)
        def _():
            chain(g, 1, 0).wait_recv()
            chain(g, 0, 1).wait_recv()
            for slot in range(2 * SIDE - 1):
                wanted = request_smem[SIDE + slot % SIDE, 0, 1 - slot // SIDE]
                upward[g][slot] = stores[g][jnp.minimum(wanted, (LAYERS - 1) * SIDE - 1)]
            chain_top(g).start()

        @pl.when(layer == LAYERS - 1)
        def _():
            chain_top(g).wait_recv()

    def hand_out(g):
        def wanted_piece(q, choice):
            wanted = request_smem[q, 0, choice]
            top = jnp.logical_and(layer == LAYERS - 1, wanted < (LAYERS - 1) * SIDE)
            return stores[g][jnp.where(top, q + SIDE * (1 - choice), wanted)]

        for offset in range(1, SIDE):
            for choice in range(2):
                piece = wanted_piece((place + offset) % SIDE, choice)
                outgoing[g][offset - 1, choice] = piece
            deliver(g, offset).start()
        for choice in range(2):
            gathered[g][1 + choice, pl.ds(place * quarter, quarter), :] = wanted_piece(
                place, choice
            )

    def compute(g):
        for c in (2 * g, 2 * g + 1):
            for offset in range(1, SIDE):
                deliver(c, offset).wait_recv()
        fetch_queries(g).wait()
        keys = gathered[2 * g][...].reshape(3 * rows, HEAD_SIZE)
        values = with_ones(gathered[2 * g + 1][...].reshape(3 * rows, HEAD_SIZE))
        for index in range(GROUP_WIDTH):
            columns = pl.ds((g * GROUP_WIDTH + index) * HEAD_SIZE, HEAD_SIZE)
            early_ref[:, columns] = attend_head(
                query_ref[:, columns], keys, values, causal, first_valid, second_valid
            )

        write_early(g).start()

    def write_early(g):
        columns = pl.ds(g * GROUP_WIDTH * HEAD_SIZE, GROUP_WIDTH * HEAD_SIZE)
        return pltpu.make_async_copy(
            early_ref.at[:, columns], early_hbm.at[:, columns], early_sem.at[g]
        )

    @pl.when(layer == 0)
    def _():
        for c in range(chunks):
            wait_spread(c)
            pass_on_low(c)

    @pl.when(layer == 1)
    def _():
        wait_spread(0)
        for c in range(chunks):
            pass_on_low(c)

    for c in range(chunks):

        @pl.when(layer >= LAYERS - 2)
        def _():
            wait_spread(c)
            pass_on_high(c)

        hand_out(c)
        if c % 2 == 1 and c > 1:
            compute(c // 2 - 1)
    for c in (chunks - 2, chunks - 1):
        for offset in range(1, SIDE):
            deliver(c, offset).wait_recv()
    for g in range(heads - 1):
        write_early(g).wait()

    for offset in range(1, SIDE):
        request(offset).wait_send()

    @pl.when(layer == LAYERS - 1)
    def _():
        for offset in range(SIDE):
            request_down(offset).wait_send()

    for g in range(chunks):
        for offset in range(1, SIDE):
            spread(g, offset).wait_send()
            deliver(g, offset).wait_send()

        @pl.when(layer == 0)
        def _():
            chain(g, 0, 0).wait_send()

        @pl.when(layer == 1)
        def _():
            chain(g, 1, 0).wait_send()
            chain(g, 0, 1).wait_send()

        @pl.when(layer == 2)
        def _():
            chain_top(g).wait_send()


def finish_kernel(
    selected_ref, query_ref, key_ref, value_ref, early_hbm, out_hbm, last_ref, early_sem, last_sem
):
    rows = query_ref.shape[0]
    early = early_hbm.shape[1]
    me = lax.axis_index("ctx")
    early_copy = pltpu.make_async_copy(early_hbm, out_hbm.at[:, pl.ds(0, early)], early_sem)
    early_copy.start()
    first_valid = selected_ref[0, 0] < me
    second_valid = jnp.logical_and(
        selected_ref[0, 1] < me, selected_ref[0, 1] != selected_ref[0, 0]
    )
    causal = lax.broadcasted_iota(jnp.int32, (rows, rows), 1) <= lax.broadcasted_iota(
        jnp.int32, (rows, rows), 0
    )
    keys = key_ref[...].reshape(3 * rows, HEAD_SIZE)
    values = with_ones(value_ref[...].reshape(3 * rows, HEAD_SIZE))
    writes = []
    for pair in range(GROUP_WIDTH // 2):
        for index in (2 * pair, 2 * pair + 1):
            columns = pl.ds(index * HEAD_SIZE, HEAD_SIZE)
            last_ref[:, columns] = attend_head(
                query_ref[:, columns], keys, values, causal, first_valid, second_valid
            )
        writes.append(
            pltpu.make_async_copy(
                last_ref.at[:, pl.ds(2 * pair * HEAD_SIZE, 2 * HEAD_SIZE)],
                out_hbm.at[:, pl.ds(early + 2 * pair * HEAD_SIZE, 2 * HEAD_SIZE)],
                last_sem.at[pair],
            )
        )
        writes[-1].start()
    for write in writes:
        write.wait()
    early_copy.wait()


def relayed(queries, all_key_states, all_value_states, selected):
    rows = queries.shape[0]
    quarter = rows // SIDE
    heads = KEY_VALUE_HEADS
    chunks = 2 * heads
    blocks = LAYERS * SIDE
    kind = all_key_states.dtype
    early = queries.shape[1] - GROUP_WIDTH * HEAD_SIZE
    vmem = pl.BlockSpec(memory_space=pltpu.VMEM)
    anywhere = pl.BlockSpec(memory_space=pl.ANY)
    dma = pltpu.SemaphoreType.DMA
    attended_early, last_keys, last_values = pl.pallas_call(
        functools.partial(relay_kernel, rows),
        out_shape=(
            jax.ShapeDtypeStruct((rows, early), queries.dtype),
            jax.ShapeDtypeStruct((3, rows, HEAD_SIZE), kind),
            jax.ShapeDtypeStruct((3, rows, HEAD_SIZE), kind),
        ),
        in_specs=[anywhere] * 4,
        out_specs=(anywhere, vmem, vmem),
        scratch_shapes=[pltpu.VMEM((blocks, quarter, HEAD_SIZE), kind)] * chunks
        + [pltpu.VMEM((2 * SIDE, quarter, HEAD_SIZE), kind)] * chunks
        + [pltpu.VMEM((SIDE - 1, 2, quarter, HEAD_SIZE), kind)] * chunks
        + [pltpu.VMEM((3, rows, HEAD_SIZE), kind)] * (chunks - 2)
        + [
            pltpu.VMEM((2 * SIDE, 1, 128), jnp.int32),
            pltpu.SMEM((2 * SIDE, 1, 128), jnp.int32),
            dma((2 * SIDE - 1,)),
            dma((2 * SIDE - 1,)),
            dma((chunks, SIDE - 1)),
            dma((chunks, SIDE - 1)),
            dma((chunks, 2)),
            dma((chunks, 2)),
            dma((chunks, SIDE - 1)),
            dma((chunks, SIDE - 1)),
            dma,
            pltpu.SMEM((1, 2), jnp.int32),
            pltpu.VMEM((rows, early), queries.dtype),
            dma,
            dma((heads - 1,)),
            dma((chunks,)),
            pltpu.VMEM((rows, early), queries.dtype),
            dma((heads - 1,)),
        ],
        compiler_params=pltpu.CompilerParams(
            collective_id=0, has_side_effects=True, vmem_limit_bytes=60 * 2**20
        ),
    )(selected, queries, all_key_states, all_value_states)
    width = GROUP_WIDTH * HEAD_SIZE
    return pl.pallas_call(
        finish_kernel,
        out_shape=jax.ShapeDtypeStruct(queries.shape, queries.dtype),
        grid=(1,),
        in_specs=[
            pl.BlockSpec(memory_space=pltpu.SMEM),
            pl.BlockSpec((rows, width), lambda i: (0, early // width)),
            pl.BlockSpec((3, rows, HEAD_SIZE), lambda i: (0, 0, 0)),
            pl.BlockSpec((3, rows, HEAD_SIZE), lambda i: (0, 0, 0)),
            anywhere,
        ],
        out_specs=anywhere,
        scratch_shapes=[
            pltpu.VMEM((rows, width), queries.dtype),
            dma,
            dma((GROUP_WIDTH // 2,)),
        ],
        compiler_params=pltpu.CompilerParams(vmem_limit_bytes=60 * 2**20),
    )(selected, queries, last_keys, last_values, attended_early)


def attend_kernel(valid_ref, query_ref, key_ref, value_ref, out_ref):
    rows = query_ref.shape[0]
    causal = lax.broadcasted_iota(jnp.int32, (rows, rows), 1) <= lax.broadcasted_iota(
        jnp.int32, (rows, rows), 0
    )
    out_ref[...] = attend_head(
        query_ref[...],
        key_ref[...],
        with_ones(value_ref[...]),
        causal,
        valid_ref[0] != 0,
        valid_ref[1] != 0,
    )


def exchanged(queries, all_key_states, all_value_states, selected):
    devices = lax.axis_size("ctx")
    me = lax.axis_index("ctx")
    rows, width = all_key_states.shape
    exchange = functools.partial(
        lax.all_to_all, axis_name="ctx", split_axis=0, concat_axis=0, tiled=True
    )
    both = jnp.concatenate([all_key_states, all_value_states], axis=1)
    requests = lax.all_gather(selected, "ctx", axis=0, tiled=True)
    held = exchange(both.reshape(devices, rows // devices, 2 * width))
    chosen = [
        exchange(jnp.take(held, requests[:, choice], axis=0)).reshape(rows, 2 * width)
        for choice in range(2)
    ]
    everything = jnp.concatenate([both] + chosen, axis=0)
    first, second = selected[0, 0], selected[0, 1]
    valid = jnp.stack([first < me, jnp.logical_and(second < me, second != first)])
    return pl.pallas_call(
        attend_kernel,
        out_shape=jax.ShapeDtypeStruct(queries.shape, queries.dtype),
        grid=(QUERY_HEADS,),
        in_specs=[
            pl.BlockSpec(memory_space=pltpu.SMEM),
            pl.BlockSpec((rows, HEAD_SIZE), lambda h: (0, h)),
            pl.BlockSpec((3 * rows, HEAD_SIZE), lambda h: (0, h // GROUP_WIDTH)),
            pl.BlockSpec((3 * rows, HEAD_SIZE), lambda h: (0, KEY_VALUE_HEADS + h // GROUP_WIDTH)),
        ],
        out_specs=pl.BlockSpec((rows, HEAD_SIZE), lambda h: (0, h)),
    )(valid.astype(jnp.int32), queries, everything, everything)


def solution(mesh):
    placed = P(("groups", "ctx"), None)
    local = relayed if mesh.shape["ctx"] == LAYERS * SIDE else exchanged
    return jax.shard_map(
        local, mesh=mesh, in_specs=(placed,) * 4, out_specs=placed, check_vma=False
    )
```

```python
import functools
import math

import jax
import jax.numpy as jnp
from jax import lax
from jax.experimental import pallas as pl
from jax.experimental.pallas import tpu as pltpu
from jax.sharding import PartitionSpec as P

QUERY_HEADS = 32
KEY_VALUE_HEADS = 4
HEAD_SIZE = 128
GROUP_WIDTH = QUERY_HEADS // KEY_VALUE_HEADS
EXPONENT_SCALE = math.log2(math.e) / math.sqrt(HEAD_SIZE)
MASKED = -1e30
LAYERS = 4
SIDE = 4
MESH = pl.DeviceIdType.MESH


def half_max(scores):
    return jnp.maximum(scores[:, :HEAD_SIZE], scores[:, HEAD_SIZE:])


def attend_head(queries, keys, values, causal, first_valid, second_valid):
    rows = queries.shape[0]
    scores = lax.dot_general(
        queries, keys, (((1,), (1,)), ((), ())), preferred_element_type=jnp.float32
    )
    own = jnp.where(causal, scores[:, :rows], MASKED)
    first = scores[:, rows : 2 * rows]
    second = scores[:, 2 * rows :]
    row_max = jnp.max(
        jnp.maximum(
            half_max(own),
            jnp.maximum(
                jnp.where(first_valid, half_max(first), MASKED),
                jnp.where(second_valid, half_max(second), MASKED),
            ),
        ),
        axis=1,
        keepdims=True,
    )
    first_max = jnp.where(first_valid, row_max, -MASKED)
    second_max = jnp.where(second_valid, row_max, -MASKED)
    weights = jnp.concatenate(
        [
            jnp.exp2((part - top) * EXPONENT_SCALE).astype(jnp.bfloat16)
            for part, top in ((own, row_max), (first, first_max), (second, second_max))
        ],
        axis=1,
    )
    mixture = jnp.dot(weights, values, preferred_element_type=jnp.float32)
    return (mixture[:, :HEAD_SIZE] * (1.0 / mixture[:, HEAD_SIZE:])).astype(jnp.bfloat16)


def with_ones(values):
    return jnp.concatenate([values, jnp.ones_like(values)], axis=1)


def relay_kernel(
    rows,
    selected_hbm,
    query_hbm,
    key_hbm,
    value_hbm,
    early_hbm,
    last_keys,
    last_values,
    *scratch,
):
    heads = KEY_VALUE_HEADS
    chunks = 2 * heads
    stores = scratch[:chunks]
    upward = scratch[chunks : 2 * chunks]
    outgoing = scratch[2 * chunks : 3 * chunks]
    gathered = scratch[3 * chunks : 4 * chunks - 2] + (last_keys, last_values)
    (
        request_vmem,
        request_smem,
        request_send,
        request_recv,
        spread_send,
        spread_recv,
        chain_send,
        chain_recv,
        deliver_send,
        deliver_recv,
        local_sem,
        selected_ref,
        query_ref,
        selected_sem,
        query_sem,
        pack_sem,
        early_ref,
        early_sem,
    ) = scratch[4 * chunks - 2 :]
    quarter = rows // SIDE
    me = lax.axis_index("ctx")
    layer = me // SIDE
    place = me % SIDE

    def peer(offset):
        return layer * SIDE + (place + offset) % SIDE

    def pack(c):
        source = (key_hbm, value_hbm)[c % 2]
        return pltpu.make_async_copy(
            source.at[:, pl.ds(c // 2 * HEAD_SIZE, HEAD_SIZE)],
            gathered[c].at[0],
            pack_sem.at[c],
        )

    def fetch_queries(g):
        columns = pl.ds(g * GROUP_WIDTH * HEAD_SIZE, GROUP_WIDTH * HEAD_SIZE)
        return pltpu.make_async_copy(
            query_hbm.at[:, columns], query_ref.at[:, columns], query_sem.at[g]
        )

    fetch_selected = pltpu.make_async_copy(selected_hbm, selected_ref, selected_sem)
    fetch_selected.start()
    for c in range(chunks):
        pack(c).start()
    for g in range(heads - 1):
        fetch_queries(g).start()

    barrier = pltpu.get_barrier_semaphore()
    for offset in range(1, SIDE):
        pl.semaphore_signal(barrier, inc=1, device_id={"ctx": peer(offset)}, device_id_type=MESH)

    @pl.when(layer > 0)
    def _():
        for q in range(SIDE):
            pl.semaphore_signal(
                barrier, inc=1, device_id={"ctx": (layer - 1) * SIDE + q}, device_id_type=MESH
            )

    @pl.when(layer < LAYERS - 1)
    def _():
        for q in range(SIDE):
            pl.semaphore_signal(
                barrier, inc=1, device_id={"ctx": (layer + 1) * SIDE + q}, device_id_type=MESH
            )

    neighbour_layers = jnp.minimum(layer, 1) + jnp.minimum(LAYERS - 1 - layer, 1)
    pl.semaphore_wait(barrier, SIDE - 1 + SIDE * neighbour_layers)

    fetch_selected.wait()
    lane = lax.broadcasted_iota(jnp.int32, (1, 128), 1)
    request_vmem[place] = jnp.where(lane == 0, selected_ref[0, 0], selected_ref[0, 1])

    def spread(g, offset):
        target = (place + offset) % SIDE
        return pltpu.make_async_remote_copy(
            src_ref=gathered[g].at[0, pl.ds(target * quarter, quarter), :],
            dst_ref=stores[g].at[me],
            send_sem=spread_send.at[g, offset - 1],
            recv_sem=spread_recv.at[g, offset - 1],
            device_id={"ctx": peer(offset)},
            device_id_type=MESH,
        )

    def request(offset):
        return pltpu.make_async_remote_copy(
            src_ref=request_vmem.at[place],
            dst_ref=request_vmem.at[place],
            send_sem=request_send.at[offset - 1],
            recv_sem=request_recv.at[offset - 1],
            device_id={"ctx": peer(offset)},
            device_id_type=MESH,
        )

    def request_down(offset):
        return pltpu.make_async_remote_copy(
            src_ref=request_vmem.at[place],
            dst_ref=request_vmem.at[SIDE + place],
            send_sem=request_send.at[SIDE - 1 + offset],
            recv_sem=request_recv.at[SIDE - 1 + offset],
            device_id={"ctx": (LAYERS - 2) * SIDE + (place + offset) % SIDE},
            device_id_type=MESH,
        )

    def chain(g, source_layer, slot):
        part = stores[g].at[pl.ds(source_layer * SIDE, SIDE)]
        return pltpu.make_async_remote_copy(
            src_ref=part,
            dst_ref=part,
            send_sem=chain_send.at[g, slot],
            recv_sem=chain_recv.at[g, slot],
            device_id={"ctx": (layer + 1) % LAYERS * SIDE + place},
            device_id_type=MESH,
        )

    def chain_top(g):
        return pltpu.make_async_remote_copy(
            src_ref=upward[g].at[pl.ds(0, 2 * SIDE - 1)],
            dst_ref=stores[g].at[pl.ds(0, 2 * SIDE - 1)],
            send_sem=chain_send.at[g, 0],
            recv_sem=chain_recv.at[g, 0],
            device_id={"ctx": (LAYERS - 1) * SIDE + place},
            device_id_type=MESH,
        )

    def deliver(g, offset):
        return pltpu.make_async_remote_copy(
            src_ref=outgoing[g].at[offset - 1],
            dst_ref=gathered[g].at[pl.ds(1, 2), pl.ds(place * quarter, quarter), :],
            send_sem=deliver_send.at[g, offset - 1],
            recv_sem=deliver_recv.at[g, offset - 1],
            device_id={"ctx": peer(offset)},
            device_id_type=MESH,
        )

    for offset in range(1, SIDE):
        request(offset).start()

    @pl.when(layer == LAYERS - 1)
    def _():
        for offset in range(SIDE):
            request_down(offset).start()

    for c in range(chunks):
        pack(c).wait()
        for offset in range(1, SIDE):
            spread(c, offset).start()
        stores[c][me] = gathered[c][0, pl.ds(place * quarter, quarter), :]

    for offset in range(1, SIDE):
        request(offset).wait_recv()

    @pl.when(layer == LAYERS - 2)
    def _():
        for offset in range(SIDE):
            request_down(offset).wait_recv()

    @pl.when(layer != LAYERS - 2)
    def _():
        for q in range(SIDE):
            request_vmem[SIDE + q] = jnp.zeros((1, 128), jnp.int32)

    to_smem = pltpu.make_async_copy(request_vmem, request_smem, local_sem)
    to_smem.start()
    to_smem.wait()

    first_valid = selected_ref[0, 0] < me
    second_valid = jnp.logical_and(
        selected_ref[0, 1] < me, selected_ref[0, 1] != selected_ref[0, 0]
    )
    causal = lax.broadcasted_iota(jnp.int32, (rows, rows), 1) <= lax.broadcasted_iota(
        jnp.int32, (rows, rows), 0
    )

    def wait_spread(g):
        for offset in range(1, SIDE):
            spread(g, offset).wait_recv()

    def pass_on_low(g):
        @pl.when(layer == 0)
        def _():
            chain(g, 0, 0).start()

        @pl.when(layer == 1)
        def _():
            if g == 0:
                chain(g, 1, 0).start()
            if g + 1 < chunks:
                wait_spread(g + 1)
                chain(g + 1, 1, 0).start()
            chain(g, 0, 0).wait_recv()
            chain(g, 0, 1).start()

    def pass_on_high(g):
        @pl.when(layer == 2)
        def _():
            chain(g, 1, 0).wait_recv()
            chain(g, 0, 1).wait_recv()
            for slot in range(2 * SIDE - 1):
                wanted = request_smem[SIDE + slot % SIDE, 0, 1 - slot // SIDE]
                upward[g][slot] = stores[g][jnp.minimum(wanted, (LAYERS - 1) * SIDE - 1)]
            chain_top(g).start()

        @pl.when(layer == LAYERS - 1)
        def _():
            chain_top(g).wait_recv()

    def hand_out(g):
        def wanted_piece(q, choice):
            wanted = request_smem[q, 0, choice]
            top = jnp.logical_and(layer == LAYERS - 1, wanted < (LAYERS - 1) * SIDE)
            return stores[g][jnp.where(top, q + SIDE * (1 - choice), wanted)]

        for offset in range(1, SIDE):
            for choice in range(2):
                piece = wanted_piece((place + offset) % SIDE, choice)
                outgoing[g][offset - 1, choice] = piece
            deliver(g, offset).start()
        for choice in range(2):
            gathered[g][1 + choice, pl.ds(place * quarter, quarter), :] = wanted_piece(
                place, choice
            )

    def compute(g):
        for c in (2 * g, 2 * g + 1):
            for offset in range(1, SIDE):
                deliver(c, offset).wait_recv()
        fetch_queries(g).wait()
        keys = gathered[2 * g][...].reshape(3 * rows, HEAD_SIZE)
        values = with_ones(gathered[2 * g + 1][...].reshape(3 * rows, HEAD_SIZE))
        for index in range(GROUP_WIDTH):
            columns = pl.ds((g * GROUP_WIDTH + index) * HEAD_SIZE, HEAD_SIZE)
            early_ref[:, columns] = attend_head(
                query_ref[:, columns], keys, values, causal, first_valid, second_valid
            )

        write_early(g).start()

    def write_early(g):
        columns = pl.ds(g * GROUP_WIDTH * HEAD_SIZE, GROUP_WIDTH * HEAD_SIZE)
        return pltpu.make_async_copy(
            early_ref.at[:, columns], early_hbm.at[:, columns], early_sem.at[g]
        )

    @pl.when(layer == 0)
    def _():
        for c in range(chunks):
            wait_spread(c)
            pass_on_low(c)

    @pl.when(layer == 1)
    def _():
        wait_spread(0)
        for c in range(chunks):
            pass_on_low(c)

    @pl.when(layer < LAYERS - 1)
    def _():
        for c in range(chunks):

            @pl.when(layer == LAYERS - 2)
            def _():
                wait_spread(c)
                pass_on_high(c)

            hand_out(c)

    for c in range(chunks):

        @pl.when(layer == LAYERS - 1)
        def _():
            wait_spread(c)
            pass_on_high(c)
            hand_out(c)

        if c % 2 == 1 and c > 1:
            compute(c // 2 - 1)

    for c in (chunks - 2, chunks - 1):
        for offset in range(1, SIDE):
            deliver(c, offset).wait_recv()
    for g in range(heads - 1):
        write_early(g).wait()

    for offset in range(1, SIDE):
        request(offset).wait_send()

    @pl.when(layer == LAYERS - 1)
    def _():
        for offset in range(SIDE):
            request_down(offset).wait_send()

    for g in range(chunks):
        for offset in range(1, SIDE):
            spread(g, offset).wait_send()
            deliver(g, offset).wait_send()

        @pl.when(layer == 0)
        def _():
            chain(g, 0, 0).wait_send()

        @pl.when(layer == 1)
        def _():
            chain(g, 1, 0).wait_send()
            chain(g, 0, 1).wait_send()

        @pl.when(layer == 2)
        def _():
            chain_top(g).wait_send()


def finish_kernel(
    selected_ref,
    query_ref,
    key_ref,
    value_ref,
    early_hbm,
    out_hbm,
    last_ref,
    early_ref,
    early_sem,
    last_sem,
):
    rows = query_ref.shape[0]
    early = early_hbm.shape[1]
    me = lax.axis_index("ctx")
    early_in = pltpu.make_async_copy(early_hbm, early_ref, early_sem.at[0])
    early_in.start()
    early_out = pltpu.make_async_copy(
        early_ref, out_hbm.at[:, pl.ds(0, early)], early_sem.at[1]
    )
    first_valid = selected_ref[0, 0] < me
    second_valid = jnp.logical_and(
        selected_ref[0, 1] < me, selected_ref[0, 1] != selected_ref[0, 0]
    )
    causal = lax.broadcasted_iota(jnp.int32, (rows, rows), 1) <= lax.broadcasted_iota(
        jnp.int32, (rows, rows), 0
    )
    keys = key_ref[...].reshape(3 * rows, HEAD_SIZE)
    values = with_ones(value_ref[...].reshape(3 * rows, HEAD_SIZE))
    writes = []
    for pair in range(GROUP_WIDTH // 2):
        for index in (2 * pair, 2 * pair + 1):
            columns = pl.ds(index * HEAD_SIZE, HEAD_SIZE)
            last_ref[:, columns] = attend_head(
                query_ref[:, columns], keys, values, causal, first_valid, second_valid
            )
        writes.append(
            pltpu.make_async_copy(
                last_ref.at[:, pl.ds(2 * pair * HEAD_SIZE, 2 * HEAD_SIZE)],
                out_hbm.at[:, pl.ds(early + 2 * pair * HEAD_SIZE, 2 * HEAD_SIZE)],
                last_sem.at[pair],
            )
        )
        writes[-1].start()
        if pair == 0:
            early_in.wait()
            early_out.start()
    for write in writes:
        write.wait()
    early_out.wait()


def relayed(queries, all_key_states, all_value_states, selected):
    rows = queries.shape[0]
    quarter = rows // SIDE
    heads = KEY_VALUE_HEADS
    chunks = 2 * heads
    blocks = LAYERS * SIDE
    kind = all_key_states.dtype
    early = queries.shape[1] - GROUP_WIDTH * HEAD_SIZE
    vmem = pl.BlockSpec(memory_space=pltpu.VMEM)
    anywhere = pl.BlockSpec(memory_space=pl.ANY)
    dma = pltpu.SemaphoreType.DMA
    attended_early, last_keys, last_values = pl.pallas_call(
        functools.partial(relay_kernel, rows),
        out_shape=(
            jax.ShapeDtypeStruct((rows, early), queries.dtype),
            jax.ShapeDtypeStruct((3, rows, HEAD_SIZE), kind),
            jax.ShapeDtypeStruct((3, rows, HEAD_SIZE), kind),
        ),
        in_specs=[anywhere] * 4,
        out_specs=(anywhere, vmem, vmem),
        scratch_shapes=[pltpu.VMEM((blocks, quarter, HEAD_SIZE), kind)] * chunks
        + [pltpu.VMEM((2 * SIDE, quarter, HEAD_SIZE), kind)] * chunks
        + [pltpu.VMEM((SIDE - 1, 2, quarter, HEAD_SIZE), kind)] * chunks
        + [pltpu.VMEM((3, rows, HEAD_SIZE), kind)] * (chunks - 2)
        + [
            pltpu.VMEM((2 * SIDE, 1, 128), jnp.int32),
            pltpu.SMEM((2 * SIDE, 1, 128), jnp.int32),
            dma((2 * SIDE - 1,)),
            dma((2 * SIDE - 1,)),
            dma((chunks, SIDE - 1)),
            dma((chunks, SIDE - 1)),
            dma((chunks, 2)),
            dma((chunks, 2)),
            dma((chunks, SIDE - 1)),
            dma((chunks, SIDE - 1)),
            dma,
            pltpu.SMEM((1, 2), jnp.int32),
            pltpu.VMEM((rows, early), queries.dtype),
            dma,
            dma((heads - 1,)),
            dma((chunks,)),
            pltpu.VMEM((rows, early), queries.dtype),
            dma((heads - 1,)),
        ],
        compiler_params=pltpu.CompilerParams(
            collective_id=0, has_side_effects=True, vmem_limit_bytes=60 * 2**20
        ),
    )(selected, queries, all_key_states, all_value_states)
    width = GROUP_WIDTH * HEAD_SIZE
    return pl.pallas_call(
        finish_kernel,
        out_shape=jax.ShapeDtypeStruct(queries.shape, queries.dtype),
        grid=(1,),
        in_specs=[
            pl.BlockSpec(memory_space=pltpu.SMEM),
            pl.BlockSpec((rows, width), lambda i: (0, early // width)),
            pl.BlockSpec((3, rows, HEAD_SIZE), lambda i: (0, 0, 0)),
            pl.BlockSpec((3, rows, HEAD_SIZE), lambda i: (0, 0, 0)),
            anywhere,
        ],
        out_specs=anywhere,
        scratch_shapes=[
            pltpu.VMEM((rows, width), queries.dtype),
            pltpu.VMEM((rows, early), queries.dtype),
            dma((2,)),
            dma((GROUP_WIDTH // 2,)),
        ],
        compiler_params=pltpu.CompilerParams(vmem_limit_bytes=60 * 2**20),
    )(selected, queries, last_keys, last_values, attended_early)


def attend_kernel(valid_ref, query_ref, key_ref, value_ref, out_ref):
    rows = query_ref.shape[0]
    causal = lax.broadcasted_iota(jnp.int32, (rows, rows), 1) <= lax.broadcasted_iota(
        jnp.int32, (rows, rows), 0
    )
    out_ref[...] = attend_head(
        query_ref[...],
        key_ref[...],
        with_ones(value_ref[...]),
        causal,
        valid_ref[0] != 0,
        valid_ref[1] != 0,
    )


def exchanged(queries, all_key_states, all_value_states, selected):
    devices = lax.axis_size("ctx")
    me = lax.axis_index("ctx")
    rows, width = all_key_states.shape
    exchange = functools.partial(
        lax.all_to_all, axis_name="ctx", split_axis=0, concat_axis=0, tiled=True
    )
    both = jnp.concatenate([all_key_states, all_value_states], axis=1)
    requests = lax.all_gather(selected, "ctx", axis=0, tiled=True)
    held = exchange(both.reshape(devices, rows // devices, 2 * width))
    chosen = [
        exchange(jnp.take(held, requests[:, choice], axis=0)).reshape(rows, 2 * width)
        for choice in range(2)
    ]
    everything = jnp.concatenate([both] + chosen, axis=0)
    first, second = selected[0, 0], selected[0, 1]
    valid = jnp.stack([first < me, jnp.logical_and(second < me, second != first)])
    return pl.pallas_call(
        attend_kernel,
        out_shape=jax.ShapeDtypeStruct(queries.shape, queries.dtype),
        grid=(QUERY_HEADS,),
        in_specs=[
            pl.BlockSpec(memory_space=pltpu.SMEM),
            pl.BlockSpec((rows, HEAD_SIZE), lambda h: (0, h)),
            pl.BlockSpec((3 * rows, HEAD_SIZE), lambda h: (0, h // GROUP_WIDTH)),
            pl.BlockSpec((3 * rows, HEAD_SIZE), lambda h: (0, KEY_VALUE_HEADS + h // GROUP_WIDTH)),
        ],
        out_specs=pl.BlockSpec((rows, HEAD_SIZE), lambda h: (0, h)),
    )(valid.astype(jnp.int32), queries, everything, everything)


def solution(mesh):
    placed = P(("groups", "ctx"), None)
    local = relayed if mesh.shape["ctx"] == LAYERS * SIDE else exchanged
    return jax.shard_map(
        local, mesh=mesh, in_specs=(placed,) * 4, out_specs=placed, check_vma=False
    )
```

```python
import functools
import math

import jax
import jax.numpy as jnp
from jax import lax
from jax.experimental import pallas as pl
from jax.experimental.pallas import tpu as pltpu
from jax.sharding import PartitionSpec as P

QUERY_HEADS = 32
KEY_VALUE_HEADS = 4
HEAD_SIZE = 128
GROUP_WIDTH = QUERY_HEADS // KEY_VALUE_HEADS
EXPONENT_SCALE = math.log2(math.e) / math.sqrt(HEAD_SIZE)
MASKED = -1e30
LAYERS = 4
SIDE = 4
AHEAD = 3
MESH = pl.DeviceIdType.MESH


def half_max(scores):
    return jnp.maximum(scores[:, :HEAD_SIZE], scores[:, HEAD_SIZE:])


def attend_head(queries, keys, values, causal, first_valid, second_valid):
    rows = queries.shape[0]
    scores = lax.dot_general(
        queries, keys, (((1,), (1,)), ((), ())), preferred_element_type=jnp.float32
    )
    own = jnp.where(causal, scores[:, :rows], MASKED)
    first = scores[:, rows : 2 * rows]
    second = scores[:, 2 * rows :]
    row_max = jnp.max(
        jnp.maximum(
            half_max(own),
            jnp.maximum(
                jnp.where(first_valid, half_max(first), MASKED),
                jnp.where(second_valid, half_max(second), MASKED),
            ),
        ),
        axis=1,
        keepdims=True,
    )
    first_max = jnp.where(first_valid, row_max, -MASKED)
    second_max = jnp.where(second_valid, row_max, -MASKED)
    weights = jnp.concatenate(
        [
            jnp.exp2((part - top) * EXPONENT_SCALE).astype(jnp.bfloat16)
            for part, top in ((own, row_max), (first, first_max), (second, second_max))
        ],
        axis=1,
    )
    mixture = jnp.dot(weights, values, preferred_element_type=jnp.float32)
    return (mixture[:, :HEAD_SIZE] * (1.0 / mixture[:, HEAD_SIZE:])).astype(jnp.bfloat16)


def with_ones(values):
    return jnp.concatenate([values, jnp.ones_like(values)], axis=1)


def relay_kernel(
    rows,
    selected_hbm,
    query_hbm,
    key_hbm,
    value_hbm,
    early_hbm,
    last_keys,
    last_values,
    *scratch,
):
    heads = KEY_VALUE_HEADS
    chunks = 2 * heads
    stores = scratch[:chunks]
    upward = scratch[chunks : 2 * chunks]
    outgoing = scratch[2 * chunks : 3 * chunks]
    gathered = scratch[3 * chunks : 4 * chunks - 2] + (last_keys, last_values)
    (
        request_vmem,
        request_smem,
        request_send,
        request_recv,
        spread_send,
        spread_recv,
        chain_send,
        chain_recv,
        deliver_send,
        deliver_recv,
        local_sem,
        selected_ref,
        query_ref,
        selected_sem,
        query_sem,
        pack_sem,
        early_ref,
        early_sem,
    ) = scratch[4 * chunks - 2 :]
    quarter = rows // SIDE
    me = lax.axis_index("ctx")
    layer = me // SIDE
    place = me % SIDE

    def peer(offset):
        return layer * SIDE + (place + offset) % SIDE

    def pack(c):
        source = (key_hbm, value_hbm)[c % 2]
        return pltpu.make_async_copy(
            source.at[:, pl.ds(c // 2 * HEAD_SIZE, HEAD_SIZE)],
            gathered[c].at[0],
            pack_sem.at[c],
        )

    def fetch_queries(g):
        columns = pl.ds(g * GROUP_WIDTH * HEAD_SIZE, GROUP_WIDTH * HEAD_SIZE)
        return pltpu.make_async_copy(
            query_hbm.at[:, columns], query_ref.at[:, columns], query_sem.at[g]
        )

    fetch_selected = pltpu.make_async_copy(selected_hbm, selected_ref, selected_sem)
    fetch_selected.start()
    for c in range(chunks):
        pack(c).start()
    for g in range(heads - 1):
        fetch_queries(g).start()

    barrier = pltpu.get_barrier_semaphore()
    for offset in range(1, SIDE):
        pl.semaphore_signal(barrier, inc=1, device_id={"ctx": peer(offset)}, device_id_type=MESH)

    @pl.when(layer > 0)
    def _():
        for q in range(SIDE):
            pl.semaphore_signal(
                barrier, inc=1, device_id={"ctx": (layer - 1) * SIDE + q}, device_id_type=MESH
            )

    @pl.when(layer < LAYERS - 1)
    def _():
        for q in range(SIDE):
            pl.semaphore_signal(
                barrier, inc=1, device_id={"ctx": (layer + 1) * SIDE + q}, device_id_type=MESH
            )

    neighbour_layers = jnp.minimum(layer, 1) + jnp.minimum(LAYERS - 1 - layer, 1)
    pl.semaphore_wait(barrier, SIDE - 1 + SIDE * neighbour_layers)

    fetch_selected.wait()
    lane = lax.broadcasted_iota(jnp.int32, (1, 128), 1)
    request_vmem[place] = jnp.where(lane == 0, selected_ref[0, 0], selected_ref[0, 1])

    def spread(g, offset):
        target = (place + offset) % SIDE
        return pltpu.make_async_remote_copy(
            src_ref=gathered[g].at[0, pl.ds(target * quarter, quarter), :],
            dst_ref=stores[g].at[me],
            send_sem=spread_send.at[g, offset - 1],
            recv_sem=spread_recv.at[g, offset - 1],
            device_id={"ctx": peer(offset)},
            device_id_type=MESH,
        )

    def request(offset):
        return pltpu.make_async_remote_copy(
            src_ref=request_vmem.at[place],
            dst_ref=request_vmem.at[place],
            send_sem=request_send.at[offset - 1],
            recv_sem=request_recv.at[offset - 1],
            device_id={"ctx": peer(offset)},
            device_id_type=MESH,
        )

    def request_down(offset):
        return pltpu.make_async_remote_copy(
            src_ref=request_vmem.at[place],
            dst_ref=request_vmem.at[SIDE + place],
            send_sem=request_send.at[SIDE - 1 + offset],
            recv_sem=request_recv.at[SIDE - 1 + offset],
            device_id={"ctx": (LAYERS - 2) * SIDE + (place + offset) % SIDE},
            device_id_type=MESH,
        )

    def chain(g, source_layer, slot):
        part = stores[g].at[pl.ds(source_layer * SIDE, SIDE)]
        return pltpu.make_async_remote_copy(
            src_ref=part,
            dst_ref=part,
            send_sem=chain_send.at[g, slot],
            recv_sem=chain_recv.at[g, slot],
            device_id={"ctx": (layer + 1) % LAYERS * SIDE + place},
            device_id_type=MESH,
        )

    def chain_top(g):
        return pltpu.make_async_remote_copy(
            src_ref=upward[g].at[pl.ds(0, 2 * SIDE - 1)],
            dst_ref=stores[g].at[pl.ds(0, 2 * SIDE - 1)],
            send_sem=chain_send.at[g, 0],
            recv_sem=chain_recv.at[g, 0],
            device_id={"ctx": (LAYERS - 1) * SIDE + place},
            device_id_type=MESH,
        )

    def deliver(g, offset):
        return pltpu.make_async_remote_copy(
            src_ref=outgoing[g].at[offset - 1],
            dst_ref=gathered[g].at[pl.ds(1, 2), pl.ds(place * quarter, quarter), :],
            send_sem=deliver_send.at[g, offset - 1],
            recv_sem=deliver_recv.at[g, offset - 1],
            device_id={"ctx": peer(offset)},
            device_id_type=MESH,
        )

    for offset in range(1, SIDE):
        request(offset).start()

    @pl.when(layer == LAYERS - 1)
    def _():
        for offset in range(SIDE):
            request_down(offset).start()

    for c in range(chunks):
        pack(c).wait()
        if c < AHEAD:
            for offset in range(1, SIDE):
                spread(c, offset).start()
        stores[c][me] = gathered[c][0, pl.ds(place * quarter, quarter), :]

    for offset in range(1, SIDE):
        request(offset).wait_recv()

    @pl.when(layer == LAYERS - 2)
    def _():
        for offset in range(SIDE):
            request_down(offset).wait_recv()

    @pl.when(layer != LAYERS - 2)
    def _():
        for q in range(SIDE):
            request_vmem[SIDE + q] = jnp.zeros((1, 128), jnp.int32)

    to_smem = pltpu.make_async_copy(request_vmem, request_smem, local_sem)
    to_smem.start()
    to_smem.wait()

    first_valid = selected_ref[0, 0] < me
    second_valid = jnp.logical_and(
        selected_ref[0, 1] < me, selected_ref[0, 1] != selected_ref[0, 0]
    )
    causal = lax.broadcasted_iota(jnp.int32, (rows, rows), 1) <= lax.broadcasted_iota(
        jnp.int32, (rows, rows), 0
    )

    def wait_spread(g):
        for offset in range(1, SIDE):
            spread(g, offset).wait_recv()
        if g + AHEAD < chunks:
            for offset in range(1, SIDE):
                spread(g + AHEAD, offset).start()

    def pass_on_low(g):
        @pl.when(layer == 0)
        def _():
            if g > 1:
                chain(g - 2, 0, 0).wait_send()
            chain(g, 0, 0).start()

        @pl.when(layer == 1)
        def _():
            if g == 0:
                chain(g, 1, 0).start()
            else:
                chain(g - 1, 1, 0).wait_send()
            if g > 1:
                chain(g - 2, 0, 1).wait_send()
            if g + 1 < chunks:
                wait_spread(g + 1)
                chain(g + 1, 1, 0).start()
            chain(g, 0, 0).wait_recv()
            chain(g, 0, 1).start()

    def pass_on_high(g):
        @pl.when(layer == 2)
        def _():
            chain(g, 1, 0).wait_recv()
            chain(g, 0, 1).wait_recv()
            for slot in range(2 * SIDE - 1):
                wanted = request_smem[SIDE + slot % SIDE, 0, 1 - slot // SIDE]
                upward[g][slot] = stores[g][jnp.minimum(wanted, (LAYERS - 1) * SIDE - 1)]
            chain_top(g).start()

        @pl.when(layer == LAYERS - 1)
        def _():
            chain_top(g).wait_recv()

    def hand_out(g):
        def wanted_piece(q, choice):
            wanted = request_smem[q, 0, choice]
            top = jnp.logical_and(layer == LAYERS - 1, wanted < (LAYERS - 1) * SIDE)
            return stores[g][jnp.where(top, q + SIDE * (1 - choice), wanted)]

        for offset in range(1, SIDE):
            for choice in range(2):
                piece = wanted_piece((place + offset) % SIDE, choice)
                outgoing[g][offset - 1, choice] = piece
            deliver(g, offset).start()
        for choice in range(2):
            gathered[g][1 + choice, pl.ds(place * quarter, quarter), :] = wanted_piece(
                place, choice
            )

    def compute(g):
        for c in (2 * g, 2 * g + 1):
            for offset in range(1, SIDE):
                deliver(c, offset).wait_recv()
        fetch_queries(g).wait()
        keys = gathered[2 * g][...].reshape(3 * rows, HEAD_SIZE)
        values = with_ones(gathered[2 * g + 1][...].reshape(3 * rows, HEAD_SIZE))
        for index in range(GROUP_WIDTH):
            columns = pl.ds((g * GROUP_WIDTH + index) * HEAD_SIZE, HEAD_SIZE)
            early_ref[:, columns] = attend_head(
                query_ref[:, columns], keys, values, causal, first_valid, second_valid
            )

        write_early(g).start()

    def write_early(g):
        columns = pl.ds(g * GROUP_WIDTH * HEAD_SIZE, GROUP_WIDTH * HEAD_SIZE)
        return pltpu.make_async_copy(
            early_ref.at[:, columns], early_hbm.at[:, columns], early_sem.at[g]
        )

    @pl.when(layer == 0)
    def _():
        for c in range(chunks):
            wait_spread(c)
            pass_on_low(c)

    @pl.when(layer == 1)
    def _():
        wait_spread(0)
        for c in range(chunks):
            pass_on_low(c)

    @pl.when(layer < LAYERS - 1)
    def _():
        for c in range(chunks):

            @pl.when(layer == LAYERS - 2)
            def _():
                wait_spread(c)
                pass_on_high(c)

            hand_out(c)

    for c in range(chunks):

        @pl.when(layer == LAYERS - 1)
        def _():
            wait_spread(c)
            pass_on_high(c)
            hand_out(c)

        if c % 2 == 1 and c > 1:
            compute(c // 2 - 1)

    for c in (chunks - 2, chunks - 1):
        for offset in range(1, SIDE):
            deliver(c, offset).wait_recv()
    for g in range(heads - 1):
        write_early(g).wait()

    for offset in range(1, SIDE):
        request(offset).wait_send()

    @pl.when(layer == LAYERS - 1)
    def _():
        for offset in range(SIDE):
            request_down(offset).wait_send()

    for g in range(chunks):
        for offset in range(1, SIDE):
            spread(g, offset).wait_send()
            deliver(g, offset).wait_send()

        @pl.when(layer == 0)
        def _():
            if g >= chunks - 2:
                chain(g, 0, 0).wait_send()

        @pl.when(layer == 1)
        def _():
            if g == chunks - 1:
                chain(g, 1, 0).wait_send()
            if g >= chunks - 2:
                chain(g, 0, 1).wait_send()

        @pl.when(layer == 2)
        def _():
            chain_top(g).wait_send()


def finish_kernel(
    selected_ref,
    query_ref,
    key_ref,
    value_ref,
    early_hbm,
    out_hbm,
    last_ref,
    early_ref,
    early_sem,
    last_sem,
):
    rows = query_ref.shape[0]
    early = early_hbm.shape[1]
    me = lax.axis_index("ctx")
    early_in = pltpu.make_async_copy(early_hbm, early_ref, early_sem.at[0])
    early_in.start()
    early_out = pltpu.make_async_copy(
        early_ref, out_hbm.at[:, pl.ds(0, early)], early_sem.at[1]
    )
    first_valid = selected_ref[0, 0] < me
    second_valid = jnp.logical_and(
        selected_ref[0, 1] < me, selected_ref[0, 1] != selected_ref[0, 0]
    )
    causal = lax.broadcasted_iota(jnp.int32, (rows, rows), 1) <= lax.broadcasted_iota(
        jnp.int32, (rows, rows), 0
    )
    keys = key_ref[...].reshape(3 * rows, HEAD_SIZE)
    values = with_ones(value_ref[...].reshape(3 * rows, HEAD_SIZE))
    writes = []
    for pair in range(GROUP_WIDTH // 2):
        for index in (2 * pair, 2 * pair + 1):
            columns = pl.ds(index * HEAD_SIZE, HEAD_SIZE)
            last_ref[:, columns] = attend_head(
                query_ref[:, columns], keys, values, causal, first_valid, second_valid
            )
        writes.append(
            pltpu.make_async_copy(
                last_ref.at[:, pl.ds(2 * pair * HEAD_SIZE, 2 * HEAD_SIZE)],
                out_hbm.at[:, pl.ds(early + 2 * pair * HEAD_SIZE, 2 * HEAD_SIZE)],
                last_sem.at[pair],
            )
        )
        writes[-1].start()
        if pair == 0:
            early_in.wait()
            early_out.start()
    for write in writes:
        write.wait()
    early_out.wait()


def relayed(queries, all_key_states, all_value_states, selected):
    rows = queries.shape[0]
    quarter = rows // SIDE
    heads = KEY_VALUE_HEADS
    chunks = 2 * heads
    blocks = LAYERS * SIDE
    kind = all_key_states.dtype
    early = queries.shape[1] - GROUP_WIDTH * HEAD_SIZE
    vmem = pl.BlockSpec(memory_space=pltpu.VMEM)
    anywhere = pl.BlockSpec(memory_space=pl.ANY)
    dma = pltpu.SemaphoreType.DMA
    attended_early, last_keys, last_values = pl.pallas_call(
        functools.partial(relay_kernel, rows),
        out_shape=(
            jax.ShapeDtypeStruct((rows, early), queries.dtype),
            jax.ShapeDtypeStruct((3, rows, HEAD_SIZE), kind),
            jax.ShapeDtypeStruct((3, rows, HEAD_SIZE), kind),
        ),
        in_specs=[anywhere] * 4,
        out_specs=(anywhere, vmem, vmem),
        scratch_shapes=[pltpu.VMEM((blocks, quarter, HEAD_SIZE), kind)] * chunks
        + [pltpu.VMEM((2 * SIDE, quarter, HEAD_SIZE), kind)] * chunks
        + [pltpu.VMEM((SIDE - 1, 2, quarter, HEAD_SIZE), kind)] * chunks
        + [pltpu.VMEM((3, rows, HEAD_SIZE), kind)] * (chunks - 2)
        + [
            pltpu.VMEM((2 * SIDE, 1, 128), jnp.int32),
            pltpu.SMEM((2 * SIDE, 1, 128), jnp.int32),
            dma((2 * SIDE - 1,)),
            dma((2 * SIDE - 1,)),
            dma((chunks, SIDE - 1)),
            dma((chunks, SIDE - 1)),
            dma((chunks, 2)),
            dma((chunks, 2)),
            dma((chunks, SIDE - 1)),
            dma((chunks, SIDE - 1)),
            dma,
            pltpu.SMEM((1, 2), jnp.int32),
            pltpu.VMEM((rows, early), queries.dtype),
            dma,
            dma((heads - 1,)),
            dma((chunks,)),
            pltpu.VMEM((rows, early), queries.dtype),
            dma((heads - 1,)),
        ],
        compiler_params=pltpu.CompilerParams(
            collective_id=0, has_side_effects=True, vmem_limit_bytes=60 * 2**20
        ),
    )(selected, queries, all_key_states, all_value_states)
    width = GROUP_WIDTH * HEAD_SIZE
    return pl.pallas_call(
        finish_kernel,
        out_shape=jax.ShapeDtypeStruct(queries.shape, queries.dtype),
        grid=(1,),
        in_specs=[
            pl.BlockSpec(memory_space=pltpu.SMEM),
            pl.BlockSpec((rows, width), lambda i: (0, early // width)),
            pl.BlockSpec((3, rows, HEAD_SIZE), lambda i: (0, 0, 0)),
            pl.BlockSpec((3, rows, HEAD_SIZE), lambda i: (0, 0, 0)),
            anywhere,
        ],
        out_specs=anywhere,
        scratch_shapes=[
            pltpu.VMEM((rows, width), queries.dtype),
            pltpu.VMEM((rows, early), queries.dtype),
            dma((2,)),
            dma((GROUP_WIDTH // 2,)),
        ],
        compiler_params=pltpu.CompilerParams(vmem_limit_bytes=60 * 2**20),
    )(selected, queries, last_keys, last_values, attended_early)


def attend_kernel(valid_ref, query_ref, key_ref, value_ref, out_ref):
    rows = query_ref.shape[0]
    causal = lax.broadcasted_iota(jnp.int32, (rows, rows), 1) <= lax.broadcasted_iota(
        jnp.int32, (rows, rows), 0
    )
    out_ref[...] = attend_head(
        query_ref[...],
        key_ref[...],
        with_ones(value_ref[...]),
        causal,
        valid_ref[0] != 0,
        valid_ref[1] != 0,
    )


def exchanged(queries, all_key_states, all_value_states, selected):
    devices = lax.axis_size("ctx")
    me = lax.axis_index("ctx")
    rows, width = all_key_states.shape
    exchange = functools.partial(
        lax.all_to_all, axis_name="ctx", split_axis=0, concat_axis=0, tiled=True
    )
    both = jnp.concatenate([all_key_states, all_value_states], axis=1)
    requests = lax.all_gather(selected, "ctx", axis=0, tiled=True)
    held = exchange(both.reshape(devices, rows // devices, 2 * width))
    chosen = [
        exchange(jnp.take(held, requests[:, choice], axis=0)).reshape(rows, 2 * width)
        for choice in range(2)
    ]
    everything = jnp.concatenate([both] + chosen, axis=0)
    first, second = selected[0, 0], selected[0, 1]
    valid = jnp.stack([first < me, jnp.logical_and(second < me, second != first)])
    return pl.pallas_call(
        attend_kernel,
        out_shape=jax.ShapeDtypeStruct(queries.shape, queries.dtype),
        grid=(QUERY_HEADS,),
        in_specs=[
            pl.BlockSpec(memory_space=pltpu.SMEM),
            pl.BlockSpec((rows, HEAD_SIZE), lambda h: (0, h)),
            pl.BlockSpec((3 * rows, HEAD_SIZE), lambda h: (0, h // GROUP_WIDTH)),
            pl.BlockSpec((3 * rows, HEAD_SIZE), lambda h: (0, KEY_VALUE_HEADS + h // GROUP_WIDTH)),
        ],
        out_specs=pl.BlockSpec((rows, HEAD_SIZE), lambda h: (0, h)),
    )(valid.astype(jnp.int32), queries, everything, everything)


def solution(mesh):
    placed = P(("groups", "ctx"), None)
    local = relayed if mesh.shape["ctx"] == LAYERS * SIDE else exchanged
    return jax.shard_map(
        local, mesh=mesh, in_specs=(placed,) * 4, out_specs=placed, check_vma=False
    )
```

```python
import functools
import math

import jax
import jax.numpy as jnp
from jax import lax
from jax.experimental import pallas as pl
from jax.experimental.pallas import tpu as pltpu
from jax.sharding import PartitionSpec as P

QUERY_HEADS = 32
KEY_VALUE_HEADS = 4
HEAD_SIZE = 128
GROUP_WIDTH = QUERY_HEADS // KEY_VALUE_HEADS
EXPONENT_SCALE = math.log2(math.e) / math.sqrt(HEAD_SIZE)
MASKED = -1e30
LAYERS = 4
SIDE = 4
MESH = pl.DeviceIdType.MESH


def half_max(scores):
    return jnp.maximum(scores[:, :HEAD_SIZE], scores[:, HEAD_SIZE:])


def attend_head(queries, keys, values, causal, first_valid, second_valid):
    rows = queries.shape[0]
    scores = lax.dot_general(
        queries, keys, (((1,), (1,)), ((), ())), preferred_element_type=jnp.float32
    )
    own = jnp.where(causal, scores[:, :rows], MASKED)
    first = scores[:, rows : 2 * rows]
    second = scores[:, 2 * rows :]
    row_max = jnp.max(
        jnp.maximum(
            half_max(own),
            jnp.maximum(
                jnp.where(first_valid, half_max(first), MASKED),
                jnp.where(second_valid, half_max(second), MASKED),
            ),
        ),
        axis=1,
        keepdims=True,
    )
    first_max = jnp.where(first_valid, row_max, -MASKED)
    second_max = jnp.where(second_valid, row_max, -MASKED)
    weights = jnp.concatenate(
        [
            jnp.exp2((part - top) * EXPONENT_SCALE).astype(jnp.bfloat16)
            for part, top in ((own, row_max), (first, first_max), (second, second_max))
        ],
        axis=1,
    )
    mixture = jnp.dot(weights, values, preferred_element_type=jnp.float32)
    return (mixture[:, :HEAD_SIZE] * (1.0 / mixture[:, HEAD_SIZE:])).astype(jnp.bfloat16)


def with_ones(values):
    return jnp.concatenate([values, jnp.ones_like(values)], axis=1)


def relay_kernel(
    rows,
    selected_hbm,
    query_hbm,
    key_hbm,
    value_hbm,
    early_hbm,
    last_keys,
    last_values,
    *scratch,
):
    heads = KEY_VALUE_HEADS
    chunks = 2 * heads
    stores = scratch[:chunks]
    upward = scratch[chunks : 2 * chunks]
    outgoing = scratch[2 * chunks : 3 * chunks]
    gathered = scratch[3 * chunks : 4 * chunks - 2] + (last_keys, last_values)
    (
        request_vmem,
        request_smem,
        request_send,
        request_recv,
        spread_send,
        spread_recv,
        chain_send,
        chain_recv,
        deliver_send,
        deliver_recv,
        local_sem,
        selected_ref,
        query_ref,
        selected_sem,
        query_sem,
        pack_sem,
        early_ref,
        early_sem,
    ) = scratch[4 * chunks - 2 :]
    quarter = rows // SIDE
    me = lax.axis_index("ctx")
    layer = me // SIDE
    place = me % SIDE

    def peer(offset):
        return layer * SIDE + (place + offset) % SIDE

    def pack(c):
        source = (key_hbm, value_hbm)[c % 2]
        return pltpu.make_async_copy(
            source.at[:, pl.ds(c // 2 * HEAD_SIZE, HEAD_SIZE)],
            gathered[c].at[0],
            pack_sem.at[c],
        )

    def fetch_queries(g):
        columns = pl.ds(g * GROUP_WIDTH * HEAD_SIZE, GROUP_WIDTH * HEAD_SIZE)
        return pltpu.make_async_copy(
            query_hbm.at[:, columns], query_ref.at[:, columns], query_sem.at[g]
        )

    fetch_selected = pltpu.make_async_copy(selected_hbm, selected_ref, selected_sem)
    fetch_selected.start()
    for c in range(chunks):
        pack(c).start()
    for g in range(heads - 1):
        fetch_queries(g).start()

    barrier = pltpu.get_barrier_semaphore()
    for offset in range(1, SIDE):
        pl.semaphore_signal(barrier, inc=1, device_id={"ctx": peer(offset)}, device_id_type=MESH)

    @pl.when(layer > 0)
    def _():
        for q in range(SIDE):
            pl.semaphore_signal(
                barrier, inc=1, device_id={"ctx": (layer - 1) * SIDE + q}, device_id_type=MESH
            )

    @pl.when(layer < LAYERS - 1)
    def _():
        for q in range(SIDE):
            pl.semaphore_signal(
                barrier, inc=1, device_id={"ctx": (layer + 1) * SIDE + q}, device_id_type=MESH
            )

    neighbour_layers = jnp.minimum(layer, 1) + jnp.minimum(LAYERS - 1 - layer, 1)
    pl.semaphore_wait(barrier, SIDE - 1 + SIDE * neighbour_layers)

    fetch_selected.wait()
    lane = lax.broadcasted_iota(jnp.int32, (1, 128), 1)
    request_vmem[place] = jnp.where(lane == 0, selected_ref[0, 0], selected_ref[0, 1])

    def spread(g, offset):
        target = (place + offset) % SIDE
        return pltpu.make_async_remote_copy(
            src_ref=gathered[g].at[0, pl.ds(target * quarter, quarter), :],
            dst_ref=stores[g].at[me],
            send_sem=spread_send.at[g, offset - 1],
            recv_sem=spread_recv.at[g, offset - 1],
            device_id={"ctx": peer(offset)},
            device_id_type=MESH,
        )

    def request(offset):
        return pltpu.make_async_remote_copy(
            src_ref=request_vmem.at[place],
            dst_ref=request_vmem.at[place],
            send_sem=request_send.at[offset - 1],
            recv_sem=request_recv.at[offset - 1],
            device_id={"ctx": peer(offset)},
            device_id_type=MESH,
        )

    def request_down(offset):
        return pltpu.make_async_remote_copy(
            src_ref=request_vmem.at[place],
            dst_ref=request_vmem.at[SIDE + place],
            send_sem=request_send.at[SIDE - 1 + offset],
            recv_sem=request_recv.at[SIDE - 1 + offset],
            device_id={"ctx": (LAYERS - 2) * SIDE + (place + offset) % SIDE},
            device_id_type=MESH,
        )

    def chain(g, source_layer, slot):
        part = stores[g].at[pl.ds(source_layer * SIDE, SIDE)]
        return pltpu.make_async_remote_copy(
            src_ref=part,
            dst_ref=part,
            send_sem=chain_send.at[g, slot],
            recv_sem=chain_recv.at[g, slot],
            device_id={"ctx": (layer + 1) % LAYERS * SIDE + place},
            device_id_type=MESH,
        )

    def chain_top(g):
        return pltpu.make_async_remote_copy(
            src_ref=upward[g].at[pl.ds(0, 2 * SIDE - 1)],
            dst_ref=stores[g].at[pl.ds(0, 2 * SIDE - 1)],
            send_sem=chain_send.at[g, 0],
            recv_sem=chain_recv.at[g, 0],
            device_id={"ctx": (LAYERS - 1) * SIDE + place},
            device_id_type=MESH,
        )

    def deliver(g, offset):
        return pltpu.make_async_remote_copy(
            src_ref=outgoing[g].at[offset - 1],
            dst_ref=gathered[g].at[pl.ds(1, 2), pl.ds(place * quarter, quarter), :],
            send_sem=deliver_send.at[g, offset - 1],
            recv_sem=deliver_recv.at[g, offset - 1],
            device_id={"ctx": peer(offset)},
            device_id_type=MESH,
        )

    for offset in range(1, SIDE):
        request(offset).start()

    @pl.when(layer == LAYERS - 1)
    def _():
        for offset in range(SIDE):
            request_down(offset).start()

    for c in range(chunks):
        pack(c).wait()
        for offset in range(1, SIDE):
            spread(c, offset).start()
        stores[c][me] = gathered[c][0, pl.ds(place * quarter, quarter), :]

    first_valid = selected_ref[0, 0] < me
    second_valid = jnp.logical_and(
        selected_ref[0, 1] < me, selected_ref[0, 1] != selected_ref[0, 0]
    )
    causal = lax.broadcasted_iota(jnp.int32, (rows, rows), 1) <= lax.broadcasted_iota(
        jnp.int32, (rows, rows), 0
    )

    def wait_spread(g):
        for offset in range(1, SIDE):
            spread(g, offset).wait_recv()

    def pass_on_low(g):
        @pl.when(layer == 0)
        def _():
            chain(g, 0, 0).start()

        @pl.when(layer == 1)
        def _():
            if g == 0:
                chain(g, 1, 0).start()
            if g + 1 < chunks:
                wait_spread(g + 1)
                chain(g + 1, 1, 0).start()
            chain(g, 0, 0).wait_recv()
            chain(g, 0, 1).start()

    def pass_on_high(g):
        @pl.when(layer == 2)
        def _():
            chain(g, 1, 0).wait_recv()
            chain(g, 0, 1).wait_recv()
            for slot in range(2 * SIDE - 1):
                wanted = request_smem[SIDE + slot % SIDE, 0, 1 - slot // SIDE]
                upward[g][slot] = stores[g][jnp.minimum(wanted, (LAYERS - 1) * SIDE - 1)]
            chain_top(g).start()

        @pl.when(layer == LAYERS - 1)
        def _():
            chain_top(g).wait_recv()

    def hand_out(g):
        def wanted_piece(q, choice):
            wanted = request_smem[q, 0, choice]
            top = jnp.logical_and(layer == LAYERS - 1, wanted < (LAYERS - 1) * SIDE)
            return stores[g][jnp.where(top, q + SIDE * (1 - choice), wanted)]

        for offset in range(1, SIDE):
            for choice in range(2):
                piece = wanted_piece((place + offset) % SIDE, choice)
                outgoing[g][offset - 1, choice] = piece
            deliver(g, offset).start()
        for choice in range(2):
            gathered[g][1 + choice, pl.ds(place * quarter, quarter), :] = wanted_piece(
                place, choice
            )

    def compute(g):
        for c in (2 * g, 2 * g + 1):
            for offset in range(1, SIDE):
                deliver(c, offset).wait_recv()
        fetch_queries(g).wait()
        keys = gathered[2 * g][...].reshape(3 * rows, HEAD_SIZE)
        values = with_ones(gathered[2 * g + 1][...].reshape(3 * rows, HEAD_SIZE))
        for index in range(GROUP_WIDTH):
            columns = pl.ds((g * GROUP_WIDTH + index) * HEAD_SIZE, HEAD_SIZE)
            early_ref[:, columns] = attend_head(
                query_ref[:, columns], keys, values, causal, first_valid, second_valid
            )

        write_early(g).start()

    def write_early(g):
        columns = pl.ds(g * GROUP_WIDTH * HEAD_SIZE, GROUP_WIDTH * HEAD_SIZE)
        return pltpu.make_async_copy(
            early_ref.at[:, columns], early_hbm.at[:, columns], early_sem.at[g]
        )

    @pl.when(layer == 0)
    def _():
        for c in range(chunks):
            wait_spread(c)
            pass_on_low(c)

    @pl.when(layer == 1)
    def _():
        wait_spread(0)
        for c in range(chunks):
            pass_on_low(c)

    for offset in range(1, SIDE):
        request(offset).wait_recv()

    @pl.when(layer == LAYERS - 2)
    def _():
        for offset in range(SIDE):
            request_down(offset).wait_recv()

    @pl.when(layer != LAYERS - 2)
    def _():
        for q in range(SIDE):
            request_vmem[SIDE + q] = jnp.zeros((1, 128), jnp.int32)

    to_smem = pltpu.make_async_copy(request_vmem, request_smem, local_sem)
    to_smem.start()
    to_smem.wait()

    @pl.when(layer < LAYERS - 1)
    def _():
        for c in range(chunks):

            @pl.when(layer == LAYERS - 2)
            def _():
                wait_spread(c)
                pass_on_high(c)

            hand_out(c)

    for c in range(chunks):

        @pl.when(layer == LAYERS - 1)
        def _():
            wait_spread(c)
            pass_on_high(c)
            hand_out(c)

        if c % 2 == 1 and c > 1:
            compute(c // 2 - 1)

    for c in (chunks - 2, chunks - 1):
        for offset in range(1, SIDE):
            deliver(c, offset).wait_recv()
    for g in range(heads - 1):
        write_early(g).wait()

    for offset in range(1, SIDE):
        request(offset).wait_send()

    @pl.when(layer == LAYERS - 1)
    def _():
        for offset in range(SIDE):
            request_down(offset).wait_send()

    for g in range(chunks):
        for offset in range(1, SIDE):
            spread(g, offset).wait_send()
            deliver(g, offset).wait_send()

        @pl.when(layer == 0)
        def _():
            chain(g, 0, 0).wait_send()

        @pl.when(layer == 1)
        def _():
            chain(g, 1, 0).wait_send()
            chain(g, 0, 1).wait_send()

        @pl.when(layer == 2)
        def _():
            chain_top(g).wait_send()


def finish_kernel(
    selected_ref,
    query_ref,
    key_ref,
    value_ref,
    early_hbm,
    out_hbm,
    last_ref,
    early_ref,
    early_sem,
    last_sem,
):
    rows = query_ref.shape[0]
    early = early_hbm.shape[1]
    me = lax.axis_index("ctx")
    early_in = pltpu.make_async_copy(early_hbm, early_ref, early_sem.at[0])
    early_in.start()
    early_out = pltpu.make_async_copy(
        early_ref, out_hbm.at[:, pl.ds(0, early)], early_sem.at[1]
    )
    first_valid = selected_ref[0, 0] < me
    second_valid = jnp.logical_and(
        selected_ref[0, 1] < me, selected_ref[0, 1] != selected_ref[0, 0]
    )
    causal = lax.broadcasted_iota(jnp.int32, (rows, rows), 1) <= lax.broadcasted_iota(
        jnp.int32, (rows, rows), 0
    )
    keys = key_ref[...].reshape(3 * rows, HEAD_SIZE)
    values = with_ones(value_ref[...].reshape(3 * rows, HEAD_SIZE))
    writes = []
    for pair in range(GROUP_WIDTH // 2):
        for index in (2 * pair, 2 * pair + 1):
            columns = pl.ds(index * HEAD_SIZE, HEAD_SIZE)
            last_ref[:, columns] = attend_head(
                query_ref[:, columns], keys, values, causal, first_valid, second_valid
            )
        writes.append(
            pltpu.make_async_copy(
                last_ref.at[:, pl.ds(2 * pair * HEAD_SIZE, 2 * HEAD_SIZE)],
                out_hbm.at[:, pl.ds(early + 2 * pair * HEAD_SIZE, 2 * HEAD_SIZE)],
                last_sem.at[pair],
            )
        )
        writes[-1].start()
        if pair == 0:
            early_in.wait()
            early_out.start()
    for write in writes:
        write.wait()
    early_out.wait()


def relayed(queries, all_key_states, all_value_states, selected):
    rows = queries.shape[0]
    quarter = rows // SIDE
    heads = KEY_VALUE_HEADS
    chunks = 2 * heads
    blocks = LAYERS * SIDE
    kind = all_key_states.dtype
    early = queries.shape[1] - GROUP_WIDTH * HEAD_SIZE
    vmem = pl.BlockSpec(memory_space=pltpu.VMEM)
    anywhere = pl.BlockSpec(memory_space=pl.ANY)
    dma = pltpu.SemaphoreType.DMA
    attended_early, last_keys, last_values = pl.pallas_call(
        functools.partial(relay_kernel, rows),
        out_shape=(
            jax.ShapeDtypeStruct((rows, early), queries.dtype),
            jax.ShapeDtypeStruct((3, rows, HEAD_SIZE), kind),
            jax.ShapeDtypeStruct((3, rows, HEAD_SIZE), kind),
        ),
        in_specs=[anywhere] * 4,
        out_specs=(anywhere, vmem, vmem),
        scratch_shapes=[pltpu.VMEM((blocks, quarter, HEAD_SIZE), kind)] * chunks
        + [pltpu.VMEM((2 * SIDE, quarter, HEAD_SIZE), kind)] * chunks
        + [pltpu.VMEM((SIDE - 1, 2, quarter, HEAD_SIZE), kind)] * chunks
        + [pltpu.VMEM((3, rows, HEAD_SIZE), kind)] * (chunks - 2)
        + [
            pltpu.VMEM((2 * SIDE, 1, 128), jnp.int32),
            pltpu.SMEM((2 * SIDE, 1, 128), jnp.int32),
            dma((2 * SIDE - 1,)),
            dma((2 * SIDE - 1,)),
            dma((chunks, SIDE - 1)),
            dma((chunks, SIDE - 1)),
            dma((chunks, 2)),
            dma((chunks, 2)),
            dma((chunks, SIDE - 1)),
            dma((chunks, SIDE - 1)),
            dma,
            pltpu.SMEM((1, 2), jnp.int32),
            pltpu.VMEM((rows, early), queries.dtype),
            dma,
            dma((heads - 1,)),
            dma((chunks,)),
            pltpu.VMEM((rows, early), queries.dtype),
            dma((heads - 1,)),
        ],
        compiler_params=pltpu.CompilerParams(
            collective_id=0, has_side_effects=True, vmem_limit_bytes=60 * 2**20
        ),
    )(selected, queries, all_key_states, all_value_states)
    width = GROUP_WIDTH * HEAD_SIZE
    return pl.pallas_call(
        finish_kernel,
        out_shape=jax.ShapeDtypeStruct(queries.shape, queries.dtype),
        grid=(1,),
        in_specs=[
            pl.BlockSpec(memory_space=pltpu.SMEM),
            pl.BlockSpec((rows, width), lambda i: (0, early // width)),
            pl.BlockSpec((3, rows, HEAD_SIZE), lambda i: (0, 0, 0)),
            pl.BlockSpec((3, rows, HEAD_SIZE), lambda i: (0, 0, 0)),
            anywhere,
        ],
        out_specs=anywhere,
        scratch_shapes=[
            pltpu.VMEM((rows, width), queries.dtype),
            pltpu.VMEM((rows, early), queries.dtype),
            dma((2,)),
            dma((GROUP_WIDTH // 2,)),
        ],
        compiler_params=pltpu.CompilerParams(vmem_limit_bytes=60 * 2**20),
    )(selected, queries, last_keys, last_values, attended_early)


def attend_kernel(valid_ref, query_ref, key_ref, value_ref, out_ref):
    rows = query_ref.shape[0]
    causal = lax.broadcasted_iota(jnp.int32, (rows, rows), 1) <= lax.broadcasted_iota(
        jnp.int32, (rows, rows), 0
    )
    out_ref[...] = attend_head(
        query_ref[...],
        key_ref[...],
        with_ones(value_ref[...]),
        causal,
        valid_ref[0] != 0,
        valid_ref[1] != 0,
    )


def exchanged(queries, all_key_states, all_value_states, selected):
    devices = lax.axis_size("ctx")
    me = lax.axis_index("ctx")
    rows, width = all_key_states.shape
    exchange = functools.partial(
        lax.all_to_all, axis_name="ctx", split_axis=0, concat_axis=0, tiled=True
    )
    both = jnp.concatenate([all_key_states, all_value_states], axis=1)
    requests = lax.all_gather(selected, "ctx", axis=0, tiled=True)
    held = exchange(both.reshape(devices, rows // devices, 2 * width))
    chosen = [
        exchange(jnp.take(held, requests[:, choice], axis=0)).reshape(rows, 2 * width)
        for choice in range(2)
    ]
    everything = jnp.concatenate([both] + chosen, axis=0)
    first, second = selected[0, 0], selected[0, 1]
    valid = jnp.stack([first < me, jnp.logical_and(second < me, second != first)])
    return pl.pallas_call(
        attend_kernel,
        out_shape=jax.ShapeDtypeStruct(queries.shape, queries.dtype),
        grid=(QUERY_HEADS,),
        in_specs=[
            pl.BlockSpec(memory_space=pltpu.SMEM),
            pl.BlockSpec((rows, HEAD_SIZE), lambda h: (0, h)),
            pl.BlockSpec((3 * rows, HEAD_SIZE), lambda h: (0, h // GROUP_WIDTH)),
            pl.BlockSpec((3 * rows, HEAD_SIZE), lambda h: (0, KEY_VALUE_HEADS + h // GROUP_WIDTH)),
        ],
        out_specs=pl.BlockSpec((rows, HEAD_SIZE), lambda h: (0, h)),
    )(valid.astype(jnp.int32), queries, everything, everything)


def solution(mesh):
    placed = P(("groups", "ctx"), None)
    local = relayed if mesh.shape["ctx"] == LAYERS * SIDE else exchanged
    return jax.shard_map(
        local, mesh=mesh, in_specs=(placed,) * 4, out_specs=placed, check_vma=False
    )
```
